256 devices in a mesh: ctx: 32 (over x_hi, z, core), tp: 8 (over x_lo, y).
Axes of the slice: x: 4 (x_hi: 2, x_lo: 2; x = x_hi * 2 + x_lo), y: 4, z: 8, core: 2. Of those that a mesh axis runs over, the one named last changes fastest.
Arguments:
- features: bfloat16 [3, 4096, 8192], P(None, 'ctx', 'tp'), may hold values from -6 to 6
- conv_weight: float32 [3, 3, 8192], replicated, may hold values from -3 to 3
- decay_rates: float32 [16, 8192], P(None, ('tp', 'ctx')), may hold values from 1e-05 to 0.03
- residues: float32 [16, 8192], P(None, ('tp', 'ctx')), may hold values from -1.5 to 1.5
- skip_gain: float32 [8192], P(('tp', 'ctx')), may hold values from -1 to 1
- out_weight: bfloat16 [8192, 8192], P('tp', 'ctx'), may hold values from -0.0625 to 0.0625
Outputs:
- mixed: bfloat16 [4096, 8192], P('ctx', 'tp')
The draws below stay inside these ranges and needn't reach their ends.
All inputs are finite; a program needn't handle non-finite values.
Results may differ from the reference program's by a relative error of at most 0.014.
Values may be sent and summed in bfloat16 or wider, within the bound.
A program may use at most 64 MiB of HBM per device.

```python
import math
import jax
import jax.numpy as jnp
from jax import lax

D = 8192
MODES = 16
SHORT = 3
SEQ = 4096
N_TP = 8


def shard_levels(stream_key, extent, shards, smallest, top_value):
    gain, own = 1.0, jax.random.fold_in(stream_key, 6)
    for dim, shards_of in shards:
        steps = jnp.exp(jax.random.uniform(jax.random.fold_in(own, dim), (shards_of,), jnp.float32, smallest / len(shards), top_value / len(shards)))
        gain = gain * jnp.repeat(steps, extent[dim] // shards_of).reshape([-1 if axis == dim else 1 for axis in range(len(extent))])
    return gain


def scatter_about(own_key, extent, scale, reach, split=(), kind=jnp.bfloat16):
    result = jax.random.normal(own_key, extent, jnp.float32) * scale
    if len(split) > 0:
        result = shard_levels(own_key, extent, split, -0.22, 0.18) * result
    return jnp.clip(result, min=-reach, max=reach).astype(kind)


def setup_inputs(seed: int = 0) -> dict:
    key_list = jax.random.split(jax.random.key(seed), 7)
    features = scatter_about(key_list[0], (3, SEQ, D), 1.0, 6.0, ((1, 32), (2, 8)))
    conv_weight = scatter_about(key_list[1], (3, SHORT, D), 0.6, 3.0, (), jnp.float32)
    decay_rates = jnp.clip(jnp.exp(math.log(0.03) - 8.006368 * jax.random.uniform(key_list[2], (MODES, D), jnp.float32) ** shard_levels(key_list[2], (MODES, D), ((1, 256),), -0.2, 0.2)), 9.999999747378752e-06, 0.03)
    residues = scatter_about(key_list[3], (MODES, D), 0.25, 1.5, ((1, 256),), jnp.float32)
    skip_gain = jnp.clip(jax.random.uniform(key_list[4], (D,), jnp.float32, -1.0, 1.0) * shard_levels(key_list[4], (D,), ((0, 256),), -0.4, 0.0), -1.0, 1.0)
    out_weight = scatter_about(key_list[5], (D, D), D ** -0.5, 0.0625, ((0, 8), (1, 32)))
    return {"features": features, "conv_weight": conv_weight, "decay_rates": decay_rates, "residues": residues, "skip_gain": skip_gain, "out_weight": out_weight}


def short_conv(signal_in, weights):
    values = signal_in.astype(jnp.float32)
    padded = jnp.pad(values, ((2, 0), (0, 0)))
    return weights[0] * values + weights[1] * padded[1:-1] + weights[2] * padded[:-2]

def filter_block(rates_block, residues_block, length):
    steps_axis = jnp.arange(length, dtype=jnp.float32)

    def add_mode(mode_index, total):
        rate_now = rates_block[mode_index][:, None]
        weight_now = residues_block[mode_index][:, None]
        return total + weight_now * jnp.sqrt(2.0 * rate_now) * jnp.exp(-rate_now * steps_axis)
    start = jnp.zeros((rates_block.shape[1], length), jnp.float32)
    return lax.fori_loop(0, rates_block.shape[0], add_mode, start)

def reference(features, conv_weight, decay_rates, residues, skip_gain, out_weight):
    query = short_conv(features[0], conv_weight[0])
    keyed = short_conv(features[1], conv_weight[1])
    valued = short_conv(features[2], conv_weight[2])
    gate_in = (keyed * valued).astype(jnp.bfloat16)
    width = gate_in.shape[1]
    length = gate_in.shape[0]
    block = math.gcd(width, 128)
    count = width // block
    channels = gate_in.astype(jnp.float32).T.reshape(count, block, length)
    rates_blocks = decay_rates.reshape(decay_rates.shape[0], count, block).transpose(1, 0, 2)
    residue_blocks = residues.reshape(residues.shape[0], count, block).transpose(1, 0, 2)

    def one_block(items):
        signal, rates_block, residues_block = items
        kernel = filter_block(rates_block, residues_block, length)
        spectrum = jnp.fft.rfft(signal, n=2 * length, axis=1) * jnp.fft.rfft(kernel, n=2 * length, axis=1)
        return jnp.fft.irfft(spectrum, n=2 * length, axis=1)[:, :length]
    convolved = lax.map(one_block, (channels, rates_blocks, residue_blocks)).reshape(width, length)
    long_out = (convolved + skip_gain[:, None] * gate_in.astype(jnp.float32).T).astype(jnp.bfloat16)
    gated = (query * long_out.T.astype(jnp.float32)).astype(jnp.bfloat16)
    share = width // N_TP
    total = jnp.zeros((length, width), jnp.float32)
    for block_index in range(N_TP):
        part = jnp.dot(gated[:, block_index * share:(block_index + 1) * share], out_weight[block_index * share:(block_index + 1) * share, :], preferred_element_type=jnp.float32).astype(jnp.bfloat16)
        part = lax.optimization_barrier(part)
        total = total + part.astype(jnp.float32)
    return total.astype(jnp.bfloat16)
```

```python
import functools

import jax
import jax.numpy as jnp
from jax import lax
from jax.experimental import pallas as pl
from jax.experimental.pallas import tpu as pltpu
from jax.sharding import PartitionSpec as P

MESH = pl.DeviceIdType.MESH
F32 = jnp.float32
BF16 = jnp.bfloat16
LANES = 128
ROWS = 8
DECAY_STEPS = 6


def row_of(tile, index):
    return jnp.broadcast_to(tile[index : index + 1, :], (ROWS, LANES))


def kernel(
    dims,
    feats,
    conv_weight,
    pack,
    weight,
    out,
    params,
    halo,
    plain,
    gate_in,
    query,
    rates,
    gains,
    skips,
    decays,
    ends,
    ends_other,
    chip_end,
    chip_ends,
    carried,
    entry,
    entry_decay,
    gated_plain,
    gated,
    weights,
    part,
    parts,
    mixed,
    pieces,
    halo_sem,
    weight_sem,
    pair_sem,
    param_send,
    param_recv,
    chip_send,
    chip_recv,
    gated_send,
    gated_recv,
    part_send,
    part_recv,
    piece_send,
    piece_recv,
):
    nz, ny, n_ctx, n_tp = dims
    per_x = 2 * nz
    modes = rates.shape[1]
    tiles = feats.shape[2] // LANES
    half_tiles = tiles // 2
    steps = feats.shape[1] // ROWS
    width = feats.shape[2]
    me = lax.axis_index("ctx")
    tp = lax.axis_index("tp")
    core = lax.rem(me, 2)
    chip = lax.div(me, 2)
    x_hi = lax.div(me, per_x)
    z = lax.rem(chip, nz)
    x_lo = lax.div(tp, ny)
    y = lax.rem(tp, ny)
    own = lax.rem(me, per_x)
    partner = me + 1 - 2 * core
    x_partner = lax.rem(me + per_x, n_ctx)
    final_tp = x_lo * ny + lax.div(z, 2)
    final_base = x_hi * per_x + 4 * y

    def remote(src, dst, send, recv, device):
        return pltpu.make_async_remote_copy(
            src_ref=src, dst_ref=dst, send_sem=send, recv_sem=recv, device_id=device, device_id_type=MESH
        )

    barrier = pltpu.get_barrier_semaphore()

    def greet_ctx(step, carry):
        pl.semaphore_signal(barrier, inc=1, device_id={"ctx": lax.rem(me + step, n_ctx)}, device_id_type=MESH)
        return carry

    def greet_tp(step, carry):
        pl.semaphore_signal(barrier, inc=1, device_id={"tp": lax.rem(tp + step, n_tp)}, device_id_type=MESH)
        return carry

    lax.fori_loop(1, n_ctx, greet_ctx, 0)
    lax.fori_loop(1, n_tp, greet_tp, 0)
    apart = final_tp != tp

    @pl.when(apart)
    def _():
        for piece in range(4):
            pl.semaphore_signal(
                barrier, inc=1, device_id={"ctx": final_base + piece, "tp": final_tp}, device_id_type=MESH
            )

    params[me] = pack[...]
    weights[x_hi] = weight[...]

    pl.semaphore_wait(barrier, n_ctx + n_tp - 2 + jnp.where(apart, 4, 0))

    last_rows = pl.ds(feats.shape[1] - halo.shape[1], halo.shape[1])

    def halo_copy(device):
        return remote(feats.at[:, last_rows, :], halo, halo_sem.at[0], halo_sem.at[1], {"ctx": device})

    def param_copy(step, source, device):
        return remote(pack, params.at[source], param_send.at[step], param_recv.at[source], {"ctx": device})

    def weight_copy(slot):
        return remote(weight, weights.at[slot], weight_sem.at[0], weight_sem.at[1], {"ctx": x_partner})

    @pl.when(me < n_ctx - 1)
    def _():
        halo_copy(me + 1).start()

    def send_params(step, carry):
        param_copy(step, me, lax.rem(me + step, n_ctx)).start()
        return carry

    lax.fori_loop(1, n_ctx, send_params, 0)
    weight_copy(x_hi).start()

    @pl.when(me > 0)
    def _():
        halo_copy(me - 1).wait_recv()

    @pl.when(me == 0)
    def _():
        halo[...] = jnp.zeros_like(halo)

    row = lax.broadcasted_iota(jnp.int32, (ROWS, LANES), 0)
    lane_group = lax.broadcasted_iota(jnp.int32, (modes, LANES), 1) // (width // n_ctx)
    groups = LANES * n_ctx // width

    def short_conv(tile, carry):
        lanes = pl.ds(pl.multiple_of(tile * LANES, LANES), LANES)
        weight_lanes = pl.ds(pl.multiple_of(tp * width + tile * LANES, LANES), LANES)
        filtered = []
        for kind in range(3):
            plain[kind] = feats[kind, :, lanes].astype(F32)
            before = halo[kind, :, lanes].astype(F32)
            taps = conv_weight[kind, :, weight_lanes]
            tap = [row_of(taps, j) for j in range(3)]
            now = [plain[kind, pl.ds(step, ROWS, stride=steps), :] for step in range(steps)]
            last = halo.shape[1] - 1
            one = jnp.where(row == 0, row_of(before, last), pltpu.roll(now[steps - 1], 1, 0))
            two = jnp.where(row == 0, row_of(before, last - 1), pltpu.roll(now[steps - 2], 1, 0))
            chain = [two, one] + now
            filtered.append(
                [tap[0] * chain[s + 2] + tap[1] * chain[s + 1] + tap[2] * chain[s] for s in range(steps)]
            )
        for step in range(steps):
            query[tile, step] = filtered[0][step]
            gate_in[tile, step] = (filtered[1][step] * filtered[2][step]).astype(BF16).astype(F32)
        return carry

    lax.fori_loop(0, tiles, short_conv, 0)

    def wait_params(step, carry):
        source = lax.rem(me + step, n_ctx)
        param_copy(step, source, source).wait_recv()
        return carry

    lax.fori_loop(1, n_ctx, wait_params, 0)

    span = width // n_ctx

    def local_states(tile, carry):
        rate = jnp.zeros((modes, LANES), F32)
        residue = jnp.zeros((modes, LANES), F32)
        skip = jnp.zeros((modes, LANES), F32)
        for group in range(groups):
            piece = params[tile * groups + group]
            at = lambda which: pltpu.roll(piece, (group - which) * span % LANES, 1)
            mine = lane_group == group
            rate = jnp.where(mine, at(0), rate)
            residue = jnp.where(mine, at(1), residue)
            skip = jnp.where(mine, at(2), skip)
        rates[tile] = rate
        gains[tile] = residue * jnp.sqrt(2.0 * rate)
        skips[tile] = skip
        power = []
        for slot, tokens in enumerate((1, steps, 2 * steps, 4 * steps, 8 * steps, 16 * steps)):
            value = jnp.exp(-float(tokens) * rate)
            power.append(value)
            decays[slot, tile] = value
        signal = [gate_in[tile, step] for step in range(steps)]
        row_tokens = row.astype(F32) * float(steps)
        for mode in range(modes):
            decay = row_of(power[0], mode)
            state = signal[0]
            for step in range(1, steps):
                state = decay * state + signal[step]
            for slot in range(3):
                reach = 1 << slot
                factor = jnp.where(row >= reach, row_of(power[1 + slot], mode), 0.0)
                state = state + factor * pltpu.roll(state, reach, 0)
            ends[tile, mode : mode + 1, :] = state[ROWS - 1 :, :]
            entry[tile, mode] = jnp.where(row >= 1, pltpu.roll(state, 1, 0), 0.0)
            entry_decay[tile, mode] = jnp.exp(-row_tokens * row_of(rate, mode))
        return carry

    lax.fori_loop(0, tiles, local_states, 0)

    pair = remote(ends, ends_other, pair_sem.at[0], pair_sem.at[1], {"ctx": partner})
    pair.start()
    pair.wait_recv()
    half = pl.ds(core * half_tiles, half_tiles)
    mine, other = ends[half], ends_other[half]
    first = jnp.where(core == 0, mine, other)
    second = jnp.where(core == 0, other, mine)
    chip_end[...] = decays[4, half] * first + second
    n_chips = n_ctx // 2

    def chip_copy(source, target):
        return remote(
            chip_end, chip_ends.at[source], chip_send.at[target], chip_recv.at[source], {"ctx": 2 * target + core}
        )

    def send_chip(target, carry):
        chip_copy(chip, target).start()
        return carry

    lax.fori_loop(chip + 1, n_chips, send_chip, 0)
    long_decay = decays[5, half]

    def take_chip(source, total):
        chip_copy(source, source).wait_recv()
        return total * long_decay + chip_ends[source]

    carried[half] = lax.fori_loop(0, chip, take_chip, jnp.zeros(chip_end.shape, F32))
    give = remote(carried.at[half], carried.at[half], pair_sem.at[2], pair_sem.at[3], {"ctx": partner})
    give.start()
    other_half = pl.ds((1 - core) * half_tiles, half_tiles)
    remote(carried.at[half], carried.at[other_half], pair_sem.at[2], pair_sem.at[3], {"ctx": partner}).wait_recv()

    def long_conv(tile, carry):
        into_chip = carried[tile]
        into = jnp.where(core == 0, into_chip, decays[4, tile] * into_chip + ends_other[tile])
        power, gain = decays[0, tile], gains[tile]
        decay = [row_of(power, m) for m in range(modes)]
        weigh = [row_of(gain, m) for m in range(modes)]
        skip = row_of(skips[tile], 0)
        state = [entry[tile, m] + entry_decay[tile, m] * row_of(into, m) for m in range(modes)]
        for step in range(steps):
            signal = gate_in[tile, step]
            total = skip * signal
            for m in range(modes):
                state[m] = decay[m] * state[m] + signal
                total = total + weigh[m] * state[m]
            long_out = total.astype(BF16).astype(F32)
            gated_plain[pl.ds(step, ROWS, stride=steps), :] = query[tile, step] * long_out
        lanes = pl.ds(pl.multiple_of(tile * LANES, LANES), LANES)
        gated[own, :, lanes] = gated_plain[...].astype(BF16)
        return carry

    lax.fori_loop(0, tiles, long_conv, 0)

    def ring_device(to_z):
        return {"ctx": x_hi * per_x + 2 * to_z + core}

    def gated_copy(block, kind, step, device):
        return remote(
            gated.at[block], gated.at[block], gated_send.at[kind, step], gated_recv.at[block], device
        )

    up = ring_device(lax.rem(z + 1, nz))
    down = ring_device(lax.rem(z + nz - 1, nz))
    across = {"ctx": partner}
    up_steps, down_steps = nz // 2, nz - 1 - nz // 2

    def part_copy(source, block, side, device):
        slot = lax.rem(block, 4)
        return remote(
            part.at[block, side],
            parts.at[source, slot],
            part_send.at[block, side],
            part_recv.at[source, slot],
            {"tp": device},
        )

    def multiply(block):
        for side in range(2):
            value = jnp.dot(gated[block], weights[side], preferred_element_type=F32).astype(BF16)
            target = side * ny + lax.div(block, 4)

            @pl.when(target == tp)
            def _():
                parts[tp, lax.rem(block, 4)] = value

            @pl.when(target != tp)
            def _():
                part[block, side] = value
                part_copy(tp, block, side, target).start()

    gated_copy(own, 0, 0, up).start()
    gated_copy(own, 1, 0, down).start()
    gated_copy(own, 2, 0, across).start()
    weight_copy(1 - x_hi).wait_recv()
    multiply(own)
    for step in range(1, up_steps + 1):
        from_down = 2 * lax.rem(z + nz - step, nz) + core
        from_up = 2 * lax.rem(z + step, nz) + core
        gated_copy(from_down, 0, 0, up).wait_recv()
        if step < up_steps:
            gated_copy(from_down, 0, step, up).start()
        gated_copy(from_down, 2, step, across).start()
        if step <= down_steps:
            gated_copy(from_up, 1, 0, down).wait_recv()
            if step < down_steps:
                gated_copy(from_up, 1, step, down).start()
            gated_copy(from_up, 3, step, across).start()
        before = step - 1
        before_down = 2 * lax.rem(z + nz - before, nz) + 1 - core
        gated_copy(before_down, 2, 0, across).wait_recv()
        multiply(before_down)
        if 0 < before <= down_steps:
            before_up = 2 * lax.rem(z + before, nz) + 1 - core
            gated_copy(before_up, 2, 0, across).wait_recv()
            multiply(before_up)
        multiply(from_down)
        if step <= down_steps:
            multiply(from_up)
    last_down = 2 * lax.rem(z + nz - up_steps, nz) + 1 - core
    gated_copy(last_down, 2, 0, across).wait_recv()
    multiply(last_down)
    if up_steps <= down_steps:
        last_up = 2 * lax.rem(z + up_steps, nz) + 1 - core
        gated_copy(last_up, 2, 0, across).wait_recv()
        multiply(last_up)

    quarter = lax.rem(me, 4)

    def piece_copy(piece, slot):
        return remote(
            mixed.at[piece],
            pieces.at[slot],
            piece_send.at[piece],
            piece_recv.at[slot],
            {"ctx": final_base + piece, "tp": final_tp},
        )

    for piece in range(4):

        def take_part(step, total):
            source = lax.rem(tp + step, n_tp)
            remote(
                part.at[0, 0], parts.at[source, piece], part_send.at[0, 0], part_recv.at[source, piece], {"tp": source}
            ).wait_recv()
            return total + parts[source, piece].astype(F32)

        value = lax.fori_loop(1, n_tp, take_part, parts[tp, piece].astype(F32)).astype(BF16)
        here = jnp.logical_and(final_base + piece == me, final_tp == tp)

        @pl.when(here)
        def _():
            pieces[quarter] = value

        @pl.when(jnp.logical_not(here))
        def _():
            mixed[piece] = value
            piece_copy(piece, quarter).start()

    cols = out.shape[1] // 4
    for piece in range(4):
        here = jnp.logical_and(final_base + piece == me, final_tp == tp)

        @pl.when(jnp.logical_not(here))
        def _():
            piece_copy(piece, piece).wait_recv()

        out[:, piece * cols : (piece + 1) * cols] = pieces[piece]

    @pl.when(me < n_ctx - 1)
    def _():
        halo_copy(me + 1).wait_send()

    def drain_params(step, carry):
        param_copy(step, me, lax.rem(me + step, n_ctx)).wait_send()
        return carry

    lax.fori_loop(1, n_ctx, drain_params, 0)
    weight_copy(x_hi).wait_send()
    pair.wait_send()
    give.wait_send()

    def drain_chip(target, carry):
        chip_copy(chip, target).wait_send()
        return carry

    lax.fori_loop(chip + 1, n_chips, drain_chip, 0)
    for step in range(up_steps):
        gated_copy(own, 0, step, up).wait_send()
    for step in range(down_steps):
        gated_copy(own, 1, step, down).wait_send()
    for step in range(up_steps + 1):
        gated_copy(own, 2, step, across).wait_send()
    for step in range(1, down_steps + 1):
        gated_copy(own, 3, step, across).wait_send()

    def drain_parts(block, carry):
        for side in range(2):
            target = side * ny + lax.div(block, 4)

            @pl.when(target != tp)
            def _():
                part_copy(tp, block, side, target).wait_send()

        return carry

    lax.fori_loop(0, per_x, drain_parts, 0)
    for piece in range(4):
        here = jnp.logical_and(final_base + piece == me, final_tp == tp)

        @pl.when(jnp.logical_not(here))
        def _():
            piece_copy(piece, quarter).wait_send()


def per_device(n_ctx, n_tp, features, conv_weight, decay_rates, residues, skip_gain, out_weight):
    nz, ny = n_ctx // 4, n_tp // 2
    _, rows, width = features.shape
    modes, span = decay_rates.shape
    skip = jnp.broadcast_to(skip_gain[None, :], (modes, span))
    fill = jnp.zeros((modes, LANES - 3 * span), F32)
    pack = jnp.concatenate([decay_rates, residues, skip, fill], axis=1)
    tiles, steps = width // LANES, rows // ROWS
    cols = out_weight.shape[1]
    blocks = 2 * nz
    tile_state = (tiles, modes, LANES)
    row_state = (tiles, modes, ROWS, LANES)
    half_state = (tiles // 2, modes, LANES)
    dma = pltpu.SemaphoreType.DMA
    vmem = pl.BlockSpec(memory_space=pltpu.VMEM)
    return pl.pallas_call(
        functools.partial(kernel, (nz, ny, n_ctx, n_tp)),
        out_shape=jax.ShapeDtypeStruct((rows, 4 * cols), BF16),
        in_specs=[vmem] * 4,
        out_specs=vmem,
        scratch_shapes=[
            pltpu.VMEM((n_ctx, modes, LANES), F32),
            pltpu.VMEM((3, 16, width), BF16),
            pltpu.VMEM((3, rows, LANES), F32),
            pltpu.VMEM((tiles, steps, ROWS, LANES), F32),
            pltpu.VMEM((tiles, steps, ROWS, LANES), F32),
            pltpu.VMEM(tile_state, F32),
            pltpu.VMEM(tile_state, F32),
            pltpu.VMEM(tile_state, F32),
            pltpu.VMEM((DECAY_STEPS,) + tile_state, F32),
            pltpu.VMEM(tile_state, F32),
            pltpu.VMEM(tile_state, F32),
            pltpu.VMEM(half_state, F32),
            pltpu.VMEM((n_ctx // 2,) + half_state, F32),
            pltpu.VMEM(tile_state, F32),
            pltpu.VMEM(row_state, F32),
            pltpu.VMEM(row_state, F32),
            pltpu.VMEM((rows, LANES), F32),
            pltpu.VMEM((blocks, rows, width), BF16),
            pltpu.VMEM((2, width, cols), BF16),
            pltpu.VMEM((blocks, 2, rows, cols), BF16),
            pltpu.VMEM((n_tp, 4, rows, cols), BF16),
            pltpu.VMEM((4, rows, cols), BF16),
            pltpu.VMEM((4, rows, cols), BF16),
            dma((2,)),
            dma((2,)),
            dma((4,)),
            dma((n_ctx,)),
            dma((n_ctx,)),
            dma((n_ctx // 2,)),
            dma((n_ctx // 2,)),
            dma((4, nz)),
            dma((blocks,)),
            dma((blocks, 2)),
            dma((n_tp, 4)),
            dma((4,)),
            dma((4,)),
        ],
        compiler_params=pltpu.CompilerParams(
            collective_id=0, has_side_effects=True, vmem_limit_bytes=48 * 1024 * 1024
        ),
    )(features, conv_weight, pack, out_weight)


def solution(mesh):
    in_specs = (
        P(None, "ctx", "tp"),
        P(),
        P(None, ("tp", "ctx")),
        P(None, ("tp", "ctx")),
        P(("tp", "ctx")),
        P("tp", "ctx"),
    )
    return jax.shard_map(
        functools.partial(per_device, mesh.shape["ctx"], mesh.shape["tp"]),
        mesh=mesh,
        in_specs=in_specs,
        out_specs=P("ctx", "tp"),
        check_vma=False,
    )
```

```python
import functools

import jax
import jax.numpy as jnp
from jax import lax
from jax.experimental import pallas as pl
from jax.experimental.pallas import tpu as pltpu
from jax.sharding import PartitionSpec as P

MESH = pl.DeviceIdType.MESH
F32 = jnp.float32
BF16 = jnp.bfloat16
LANES = 128
ROWS = 8
CROSS_LAG = 3
STRIP_LAG = 6
DECAY_STEPS = 6


def row_of(tile, index):
    return jnp.broadcast_to(tile[index : index + 1, :], (ROWS, LANES))


def kernel(
    dims,
    feats,
    conv_weight,
    pack,
    weight,
    out,
    params,
    halo,
    plain,
    gate_in,
    query,
    rates,
    gains,
    skips,
    decays,
    ends,
    ends_other,
    chip_end,
    chip_ends,
    carried,
    entry,
    entry_decay,
    gated_plain,
    gated,
    weights,
    kept,
    crossing,
    crossed,
    summed,
    strips,
    mixed,
    pieces,
    halo_sem,
    weight_sem,
    pair_sem,
    param_send,
    param_recv,
    chip_send,
    chip_recv,
    ring_send,
    across_send,
    gated_recv,
    cross_send,
    cross_recv,
    strip_send,
    strip_recv,
    piece_send,
    piece_recv,
):
    nz, ny, n_ctx, n_tp = dims
    per_x = 2 * nz
    modes = rates.shape[1]
    tiles = feats.shape[2] // LANES
    half_tiles = tiles // 2
    steps = feats.shape[1] // ROWS
    width = feats.shape[2]
    me = lax.axis_index("ctx")
    tp = lax.axis_index("tp")
    core = lax.rem(me, 2)
    chip = lax.div(me, 2)
    x_hi = lax.div(me, per_x)
    z = lax.rem(chip, nz)
    x_lo = lax.div(tp, ny)
    y = lax.rem(tp, ny)
    own = lax.rem(me, per_x)
    partner = me + 1 - 2 * core
    x_partner = lax.rem(me + per_x, n_ctx)
    final_y = lax.div(z, 2)
    quarter = lax.rem(me, 4)
    strip_rows = feats.shape[1] // ny

    def remote(src, dst, send, recv, device):
        return pltpu.make_async_remote_copy(
            src_ref=src, dst_ref=dst, send_sem=send, recv_sem=recv, device_id=device, device_id_type=MESH
        )

    barrier = pltpu.get_barrier_semaphore()

    def greet_ctx(step, carry):
        pl.semaphore_signal(barrier, inc=1, device_id={"ctx": lax.rem(me + step, n_ctx)}, device_id_type=MESH)
        return carry

    def greet_tp(step, carry):
        pl.semaphore_signal(barrier, inc=1, device_id={"tp": lax.rem(tp + step, n_tp)}, device_id_type=MESH)
        return carry

    lax.fori_loop(1, n_ctx, greet_ctx, 0)
    lax.fori_loop(1, n_tp, greet_tp, 0)
    for other_y in range(1, ny):
        for which in range(4):
            pl.semaphore_signal(
                barrier,
                inc=1,
                device_id={"ctx": x_hi * per_x + 4 * y + which, "tp": x_lo * ny + lax.rem(y + other_y, ny)},
                device_id_type=MESH,
            )

    params[me] = pack[...]
    weights[x_hi] = weight[...]

    pl.semaphore_wait(barrier, n_ctx + n_tp - 2 + jnp.where(final_y != y, per_x, 0))

    last_rows = pl.ds(feats.shape[1] - halo.shape[1], halo.shape[1])

    def halo_copy(device):
        return remote(feats.at[:, last_rows, :], halo, halo_sem.at[0], halo_sem.at[1], {"ctx": device})

    def param_copy(step, source, device):
        return remote(pack, params.at[source], param_send.at[step], param_recv.at[source], {"ctx": device})

    def weight_copy(slot):
        return remote(weight, weights.at[slot], weight_sem.at[0], weight_sem.at[1], {"ctx": x_partner})

    @pl.when(me < n_ctx - 1)
    def _():
        halo_copy(me + 1).start()

    def send_params(step, carry):
        param_copy(step, me, lax.rem(me + step, n_ctx)).start()
        return carry

    lax.fori_loop(1, n_ctx, send_params, 0)
    weight_copy(x_hi).start()

    @pl.when(me > 0)
    def _():
        halo_copy(me - 1).wait_recv()

    @pl.when(me == 0)
    def _():
        halo[...] = jnp.zeros_like(halo)

    row = lax.broadcasted_iota(jnp.int32, (ROWS, LANES), 0)
    lane_group = lax.broadcasted_iota(jnp.int32, (modes, LANES), 1) // (width // n_ctx)
    groups = LANES * n_ctx // width

    def short_conv(tile, carry):
        lanes = pl.ds(pl.multiple_of(tile * LANES, LANES), LANES)
        weight_lanes = pl.ds(pl.multiple_of(tp * width + tile * LANES, LANES), LANES)
        filtered = []
        for kind in range(3):
            plain[kind] = feats[kind, :, lanes].astype(F32)
            before = halo[kind, :, lanes].astype(F32)
            taps = conv_weight[kind, :, weight_lanes]
            tap = [row_of(taps, j) for j in range(3)]
            now = [plain[kind, pl.ds(step, ROWS, stride=steps), :] for step in range(steps)]
            last = halo.shape[1] - 1
            one = jnp.where(row == 0, row_of(before, last), pltpu.roll(now[steps - 1], 1, 0))
            two = jnp.where(row == 0, row_of(before, last - 1), pltpu.roll(now[steps - 2], 1, 0))
            chain = [two, one] + now
            filtered.append(
                [tap[0] * chain[s + 2] + tap[1] * chain[s + 1] + tap[2] * chain[s] for s in range(steps)]
            )
        for step in range(steps):
            query[tile, step] = filtered[0][step]
            gate_in[tile, step] = (filtered[1][step] * filtered[2][step]).astype(BF16).astype(F32)
        return carry

    lax.fori_loop(0, tiles, short_conv, 0)

    def wait_params(step, carry):
        source = lax.rem(me + step, n_ctx)
        param_copy(step, source, source).wait_recv()
        return carry

    lax.fori_loop(1, n_ctx, wait_params, 0)

    span = width // n_ctx

    def local_states(tile, carry):
        rate = jnp.zeros((modes, LANES), F32)
        residue = jnp.zeros((modes, LANES), F32)
        skip = jnp.zeros((modes, LANES), F32)
        for group in range(groups):
            piece = params[tile * groups + group]
            at = lambda which: pltpu.roll(piece, (group - which) * span % LANES, 1)
            mine = lane_group == group
            rate = jnp.where(mine, at(0), rate)
            residue = jnp.where(mine, at(1), residue)
            skip = jnp.where(mine, at(2), skip)
        rates[tile] = rate
        gains[tile] = residue * jnp.sqrt(2.0 * rate)
        skips[tile] = skip
        power = []
        for slot, tokens in enumerate((1, steps, 2 * steps, 4 * steps, 8 * steps, 16 * steps)):
            value = jnp.exp(-float(tokens) * rate)
            power.append(value)
            decays[slot, tile] = value
        signal = [gate_in[tile, step] for step in range(steps)]
        row_tokens = row.astype(F32) * float(steps)
        for mode in range(modes):
            decay = row_of(power[0], mode)
            state = signal[0]
            for step in range(1, steps):
                state = decay * state + signal[step]
            for slot in range(3):
                reach = 1 << slot
                factor = jnp.where(row >= reach, row_of(power[1 + slot], mode), 0.0)
                state = state + factor * pltpu.roll(state, reach, 0)
            ends[tile, mode : mode + 1, :] = state[ROWS - 1 :, :]
            entry[tile, mode] = jnp.where(row >= 1, pltpu.roll(state, 1, 0), 0.0)
            entry_decay[tile, mode] = jnp.exp(-row_tokens * row_of(rate, mode))
        return carry

    lax.fori_loop(0, tiles, local_states, 0)

    pair = remote(ends, ends_other, pair_sem.at[0], pair_sem.at[1], {"ctx": partner})
    pair.start()
    pair.wait_recv()
    half = pl.ds(core * half_tiles, half_tiles)
    mine, other = ends[half], ends_other[half]
    first = jnp.where(core == 0, mine, other)
    second = jnp.where(core == 0, other, mine)
    chip_end[...] = decays[4, half] * first + second
    n_chips = n_ctx // 2

    def chip_copy(source, target):
        return remote(
            chip_end, chip_ends.at[source], chip_send.at[target], chip_recv.at[source], {"ctx": 2 * target + core}
        )

    def send_chip(target, carry):
        chip_copy(chip, target).start()
        return carry

    lax.fori_loop(chip + 1, n_chips, send_chip, 0)
    long_decay = decays[5, half]

    def take_chip(source, total):
        chip_copy(source, source).wait_recv()
        return total * long_decay + chip_ends[source]

    carried[half] = lax.fori_loop(0, chip, take_chip, jnp.zeros(chip_end.shape, F32))
    give = remote(carried.at[half], carried.at[half], pair_sem.at[2], pair_sem.at[3], {"ctx": partner})
    give.start()
    other_half = pl.ds((1 - core) * half_tiles, half_tiles)
    remote(carried.at[half], carried.at[other_half], pair_sem.at[2], pair_sem.at[3], {"ctx": partner}).wait_recv()

    def long_conv(tile, carry):
        into_chip = carried[tile]
        into = jnp.where(core == 0, into_chip, decays[4, tile] * into_chip + ends_other[tile])
        power, gain = decays[0, tile], gains[tile]
        decay = [row_of(power, m) for m in range(modes)]
        weigh = [row_of(gain, m) for m in range(modes)]
        skip = row_of(skips[tile], 0)
        state = [entry[tile, m] + entry_decay[tile, m] * row_of(into, m) for m in range(modes)]
        for step in range(steps):
            signal = gate_in[tile, step]
            total = skip * signal
            for m in range(modes):
                state[m] = decay[m] * state[m] + signal
                total = total + weigh[m] * state[m]
            long_out = total.astype(BF16).astype(F32)
            gated_plain[pl.ds(step, ROWS, stride=steps), :] = query[tile, step] * long_out
        lanes = pl.ds(pl.multiple_of(tile * LANES, LANES), LANES)
        gated[own, :, lanes] = gated_plain[...].astype(BF16)
        return carry

    lax.fori_loop(0, tiles, long_conv, 0)

    def ring_device(to_z):
        return {"ctx": x_hi * per_x + 2 * to_z + core}

    devices = [ring_device(lax.rem(z + 1, nz)), ring_device(lax.rem(z + nz - 1, nz))]
    far = nz // 2
    half_rows = feats.shape[1] // 2

    def ring_halves(way, step):
        return [way, 1 - way] if step < far else [way]

    def ring_block(way, step):
        return 2 * lax.rem(z + (nz - step if way == 0 else step), nz) + core

    def ring_copy(block, way, step, part):
        rows = pl.ds(part * half_rows, half_rows)
        return remote(
            gated.at[block, rows],
            gated.at[block, rows],
            ring_send.at[way, step, part],
            gated_recv.at[block, part],
            devices[way],
        )

    def across_copy(block, slot):
        return remote(
            gated.at[block], gated.at[block], across_send.at[slot], gated_recv.at[block, 0], {"ctx": partner}
        )

    def cross_copy(block):
        return remote(
            crossing.at[block],
            crossed.at[block],
            cross_send.at[block],
            cross_recv.at[block],
            {"tp": (1 - x_lo) * ny + y},
        )

    def strip_copy(block, source, target):
        rows = pl.ds(pl.multiple_of(target * strip_rows, strip_rows), strip_rows)
        return remote(
            summed.at[block, rows],
            strips.at[source, block],
            strip_send.at[block, target],
            strip_recv.at[source, block],
            {"tp": x_lo * ny + target},
        )

    def piece_copy(block, which, strip):
        rows = pl.ds(pl.multiple_of(strip * strip_rows, strip_rows), strip_rows)
        return remote(
            mixed.at[block],
            pieces.at[which, rows],
            piece_send.at[block],
            piece_recv.at[which, strip],
            {"ctx": x_hi * per_x + block, "tp": x_lo * ny + final_y},
        )

    def stays(block):
        return jnp.logical_and(block == own, final_y == y)

    def multiply(block):
        value = jnp.dot(gated[block], weights[1 - x_lo], preferred_element_type=F32)
        crossing[block] = value.astype(BF16)
        cross_copy(block).start()
        kept[block] = jnp.dot(gated[block], weights[x_lo], preferred_element_type=F32)

    def combine(block):
        cross_copy(block).wait_recv()
        summed[block] = (kept[block] + crossed[block].astype(F32)).astype(BF16)
        for step in range(1, ny):
            strip_copy(block, y, lax.rem(y + step, ny)).start()

    def finish(block):
        own_rows = pl.ds(pl.multiple_of(y * strip_rows, strip_rows), strip_rows)
        total = summed[block, own_rows].astype(F32)
        for step in range(1, ny):
            source = lax.rem(y + step, ny)
            strip_copy(block, source, y).wait_recv()
            total = total + strips[source, block].astype(F32)
        value = total.astype(BF16)

        @pl.when(stays(block))
        def _():
            pieces[quarter, own_rows] = value

        @pl.when(jnp.logical_not(stays(block)))
        def _():
            mixed[block] = value
            piece_copy(block, quarter, y).start()

    for way in range(2):
        for part in ring_halves(way, 1):
            ring_copy(own, way, 0, part).start()
    across_copy(own, 0).start()
    weight_copy(1 - x_hi).wait_recv()

    done = []

    def advance(entry):
        block, waits = entry
        if waits:
            across_copy(block, 0).wait_recv()
        multiply(block)
        done.append(block)
        if len(done) > CROSS_LAG:
            combine(done[-1 - CROSS_LAG])
        if len(done) > STRIP_LAG:
            finish(done[-1 - STRIP_LAG])

    def other(block):
        return block + 1 - 2 * core

    pending = [(own, False)]
    later = [(other(own), True)]
    for step in range(1, far + 1):
        ways = [0, 1]
        arrived = [ring_block(way, step) for way in ways]
        for turn in range(len(ring_halves(0, step))):
            for way in ways:
                part = ring_halves(way, step)[turn]
                ring_copy(arrived[way], way, 0, part).wait_recv()
                if step < far and part in ring_halves(way, step + 1):
                    ring_copy(arrived[way], way, step, part).start()
            if turn == 0:
                for _ in range(min(2, len(pending))):
                    advance(pending.pop(0))
        blocks = arrived if step < far else arrived[:1]
        for index, block in enumerate(blocks):
            across_copy(block, 2 * step - 1 + index).start()
        while pending:
            advance(pending.pop(0))
        pending = later + [(block, False) for block in blocks]
        later = [(other(block), True) for block in blocks]
    for entry_left in pending + later:
        advance(entry_left)
    total_blocks = len(done)
    for index in range(total_blocks - CROSS_LAG, total_blocks):
        combine(done[index])
    for index in range(total_blocks - STRIP_LAG, total_blocks):
        finish(done[index])

    cols = out.shape[1] // 4
    for which in range(4):
        for strip in range(ny):
            here = jnp.logical_and(jnp.logical_and(final_y == y, quarter == which), y == strip)

            @pl.when(jnp.logical_not(here))
            def _():
                piece_copy(own, which, strip).wait_recv()

        out[:, which * cols : (which + 1) * cols] = pieces[which]

    @pl.when(me < n_ctx - 1)
    def _():
        halo_copy(me + 1).wait_send()

    def drain_params(step, carry):
        param_copy(step, me, lax.rem(me + step, n_ctx)).wait_send()
        return carry

    lax.fori_loop(1, n_ctx, drain_params, 0)
    weight_copy(x_hi).wait_send()
    pair.wait_send()
    give.wait_send()

    def drain_chip(target, carry):
        chip_copy(chip, target).wait_send()
        return carry

    lax.fori_loop(chip + 1, n_chips, drain_chip, 0)
    for step in range(far):
        for way in range(2):
            for part in ring_halves(way, step + 1):
                ring_copy(own, way, step, part).wait_send()
    for slot in range(nz):
        across_copy(own, slot).wait_send()

    def drain_blocks(block, carry):
        cross_copy(block).wait_send()
        for step in range(1, ny):
            strip_copy(block, y, lax.rem(y + step, ny)).wait_send()

        @pl.when(jnp.logical_not(stays(block)))
        def _():
            piece_copy(block, quarter, y).wait_send()

        return carry

    lax.fori_loop(0, per_x, drain_blocks, 0)


def per_device(n_ctx, n_tp, features, conv_weight, decay_rates, residues, skip_gain, out_weight):
    nz, ny = n_ctx // 4, n_tp // 2
    _, rows, width = features.shape
    modes, span = decay_rates.shape
    skip = jnp.broadcast_to(skip_gain[None, :], (modes, span))
    fill = jnp.zeros((modes, LANES - 3 * span), F32)
    pack = jnp.concatenate([decay_rates, residues, skip, fill], axis=1)
    tiles, steps = width // LANES, rows // ROWS
    cols = out_weight.shape[1]
    blocks = 2 * nz
    tile_state = (tiles, modes, LANES)
    row_state = (tiles, modes, ROWS, LANES)
    half_state = (tiles // 2, modes, LANES)
    dma = pltpu.SemaphoreType.DMA
    vmem = pl.BlockSpec(memory_space=pltpu.VMEM)
    return pl.pallas_call(
        functools.partial(kernel, (nz, ny, n_ctx, n_tp)),
        out_shape=jax.ShapeDtypeStruct((rows, 4 * cols), BF16),
        in_specs=[vmem] * 4,
        out_specs=vmem,
        scratch_shapes=[
            pltpu.VMEM((n_ctx, modes, LANES), F32),
            pltpu.VMEM((3, 16, width), BF16),
            pltpu.VMEM((3, rows, LANES), F32),
            pltpu.VMEM((tiles, steps, ROWS, LANES), F32),
            pltpu.VMEM((tiles, steps, ROWS, LANES), F32),
            pltpu.VMEM(tile_state, F32),
            pltpu.VMEM(tile_state, F32),
            pltpu.VMEM(tile_state, F32),
            pltpu.VMEM((DECAY_STEPS,) + tile_state, F32),
            pltpu.VMEM(tile_state, F32),
            pltpu.VMEM(tile_state, F32),
            pltpu.VMEM(half_state, F32),
            pltpu.VMEM((n_ctx // 2,) + half_state, F32),
            pltpu.VMEM(tile_state, F32),
            pltpu.VMEM(row_state, F32),
            pltpu.VMEM(row_state, F32),
            pltpu.VMEM((rows, LANES), F32),
            pltpu.VMEM((blocks, rows, width), BF16),
            pltpu.VMEM((2, width, cols), BF16),
            pltpu.VMEM((blocks, rows, cols), F32),
            pltpu.VMEM((blocks, rows, cols), BF16),
            pltpu.VMEM((blocks, rows, cols), BF16),
            pltpu.VMEM((blocks, rows, cols), BF16),
            pltpu.VMEM((ny, blocks, rows // ny, cols), BF16),
            pltpu.VMEM((blocks, rows // ny, cols), BF16),
            pltpu.VMEM((4, rows, cols), BF16),
            dma((2,)),
            dma((2,)),
            dma((4,)),
            dma((n_ctx,)),
            dma((n_ctx,)),
            dma((n_ctx // 2,)),
            dma((n_ctx // 2,)),
            dma((2, nz // 2, 2)),
            dma((nz,)),
            dma((blocks, 2)),
            dma((blocks,)),
            dma((blocks,)),
            dma((blocks, ny)),
            dma((ny, blocks)),
            dma((blocks,)),
            dma((4, ny)),
        ],
        compiler_params=pltpu.CompilerParams(
            collective_id=0, has_side_effects=True, vmem_limit_bytes=48 * 1024 * 1024
        ),
    )(features, conv_weight, pack, out_weight)


def solution(mesh):
    in_specs = (
        P(None, "ctx", "tp"),
        P(),
        P(None, ("tp", "ctx")),
        P(None, ("tp", "ctx")),
        P(("tp", "ctx")),
        P("tp", "ctx"),
    )
    return jax.shard_map(
        functools.partial(per_device, mesh.shape["ctx"], mesh.shape["tp"]),
        mesh=mesh,
        in_specs=in_specs,
        out_specs=P("ctx", "tp"),
        check_vma=False,
    )
```

```python
import functools

import jax
import jax.numpy as jnp
from jax import lax
from jax.experimental import pallas as pl
from jax.experimental.pallas import tpu as pltpu
from jax.sharding import PartitionSpec as P

MESH = pl.DeviceIdType.MESH
F32 = jnp.float32
BF16 = jnp.bfloat16
LANES = 128
ROWS = 8
CROSS_LAG = 3
STRIP_LAG = 6
DECAY_STEPS = 6


def row_of(tile, index):
    return jnp.broadcast_to(tile[index : index + 1, :], (ROWS, LANES))


def kernel(
    dims,
    features,
    all_taps,
    decay_rates,
    residues,
    skip_gain,
    weight,
    out,
    feats,
    conv_weight,
    own_rates,
    own_residues,
    own_skip,
    pack,
    params,
    halo,
    plain,
    gate_in,
    query,
    rates,
    gains,
    skips,
    decays,
    ends,
    ends_other,
    chip_end,
    chip_ends,
    carried,
    entry,
    entry_decay,
    gated_plain,
    gated,
    weights,
    kept,
    crossing,
    crossed,
    summed,
    strips,
    mixed,
    pieces,
    fetch_sem,
    halo_sem,
    weight_sem,
    pair_sem,
    param_send,
    param_recv,
    chip_send,
    chip_recv,
    ring_send,
    across_send,
    gated_recv,
    cross_send,
    cross_recv,
    strip_send,
    strip_recv,
    piece_send,
    piece_recv,
):
    nz, ny, n_ctx, n_tp = dims
    per_x = 2 * nz
    modes = rates.shape[1]
    tiles = feats.shape[2] // LANES
    half_tiles = tiles // 2
    steps = feats.shape[1] // ROWS
    width = feats.shape[2]
    me = lax.axis_index("ctx")
    tp = lax.axis_index("tp")
    core = lax.rem(me, 2)
    chip = lax.div(me, 2)
    x_hi = lax.div(me, per_x)
    z = lax.rem(chip, nz)
    x_lo = lax.div(tp, ny)
    y = lax.rem(tp, ny)
    own = lax.rem(me, per_x)
    partner = me + 1 - 2 * core
    x_partner = lax.rem(me + per_x, n_ctx)
    final_y = lax.div(z, 2)
    quarter = lax.rem(me, 4)
    strip_rows = feats.shape[1] // ny

    def remote(src, dst, send, recv, device):
        return pltpu.make_async_remote_copy(
            src_ref=src, dst_ref=dst, send_sem=send, recv_sem=recv, device_id=device, device_id_type=MESH
        )

    own_lanes = pl.ds(pl.multiple_of(tp * width, width), width)
    fetches = [
        pltpu.make_async_copy(src, dst, fetch_sem.at[slot])
        for slot, (src, dst) in enumerate(
            [
                (decay_rates, own_rates),
                (residues, own_residues),
                (skip_gain, own_skip),
                (features, feats),
                (all_taps.at[:, :, own_lanes], conv_weight),
                (weight, weights.at[x_hi]),
            ]
        )
    ]
    for fetch in fetches:
        fetch.start()

    barrier = pltpu.get_barrier_semaphore()

    def greet_ctx(step, carry):
        pl.semaphore_signal(barrier, inc=1, device_id={"ctx": lax.rem(me + step, n_ctx)}, device_id_type=MESH)
        return carry

    def greet_tp(step, carry):
        pl.semaphore_signal(barrier, inc=1, device_id={"tp": lax.rem(tp + step, n_tp)}, device_id_type=MESH)
        return carry

    lax.fori_loop(1, n_ctx, greet_ctx, 0)
    lax.fori_loop(1, n_tp, greet_tp, 0)
    for other_y in range(1, ny):
        for which in range(4):
            pl.semaphore_signal(
                barrier,
                inc=1,
                device_id={"ctx": x_hi * per_x + 4 * y + which, "tp": x_lo * ny + lax.rem(y + other_y, ny)},
                device_id_type=MESH,
            )

    for fetch in fetches:
        fetch.wait()
    modes_shape = own_rates.shape
    packed = jnp.concatenate(
        [
            own_rates[...],
            own_residues[...],
            jnp.broadcast_to(own_skip[...], modes_shape),
            jnp.zeros((modes_shape[0], LANES - 3 * modes_shape[1]), F32),
        ],
        axis=1,
    )
    pack[...] = packed
    params[me] = packed

    pl.semaphore_wait(barrier, n_ctx + n_tp - 2 + jnp.where(final_y != y, per_x, 0))

    last_rows = pl.ds(feats.shape[1] - halo.shape[1], halo.shape[1])

    def halo_copy(device):
        return remote(feats.at[:, last_rows, :], halo, halo_sem.at[0], halo_sem.at[1], {"ctx": device})

    def param_copy(step, source, device):
        return remote(pack, params.at[source], param_send.at[step], param_recv.at[source], {"ctx": device})

    def weight_copy(slot):
        return remote(weights.at[slot], weights.at[slot], weight_sem.at[0], weight_sem.at[1], {"ctx": x_partner})

    @pl.when(me < n_ctx - 1)
    def _():
        halo_copy(me + 1).start()

    def send_params(step, carry):
        param_copy(step, me, lax.rem(me + step, n_ctx)).start()
        return carry

    lax.fori_loop(1, n_ctx, send_params, 0)

    @pl.when(me > 0)
    def _():
        halo_copy(me - 1).wait_recv()

    @pl.when(me == 0)
    def _():
        halo[...] = jnp.zeros_like(halo)

    row = lax.broadcasted_iota(jnp.int32, (ROWS, LANES), 0)
    lane_group = lax.broadcasted_iota(jnp.int32, (modes, LANES), 1) // (width // n_ctx)
    groups = LANES * n_ctx // width

    def short_conv(tile, carry):
        lanes = pl.ds(pl.multiple_of(tile * LANES, LANES), LANES)
        filtered = []
        for kind in range(3):
            plain[kind] = feats[kind, :, lanes].astype(F32)
            before = halo[kind, :, lanes].astype(F32)
            taps = conv_weight[kind, :, lanes]
            tap = [row_of(taps, j) for j in range(3)]
            now = [plain[kind, pl.ds(step, ROWS, stride=steps), :] for step in range(steps)]
            last = halo.shape[1] - 1
            one = jnp.where(row == 0, row_of(before, last), pltpu.roll(now[steps - 1], 1, 0))
            two = jnp.where(row == 0, row_of(before, last - 1), pltpu.roll(now[steps - 2], 1, 0))
            chain = [two, one] + now
            filtered.append(
                [tap[0] * chain[s + 2] + tap[1] * chain[s + 1] + tap[2] * chain[s] for s in range(steps)]
            )
        for step in range(steps):
            query[tile, step] = filtered[0][step]
            gate_in[tile, step] = (filtered[1][step] * filtered[2][step]).astype(BF16).astype(F32)
        return carry

    lax.fori_loop(0, tiles, short_conv, 0)

    def wait_params(step, carry):
        source = lax.rem(me + step, n_ctx)
        param_copy(step, source, source).wait_recv()
        return carry

    lax.fori_loop(1, n_ctx, wait_params, 0)
    weight_copy(x_hi).start()

    span = width // n_ctx

    def local_states(tile, carry):
        rate = jnp.zeros((modes, LANES), F32)
        residue = jnp.zeros((modes, LANES), F32)
        skip = jnp.zeros((modes, LANES), F32)
        for group in range(groups):
            piece = params[tile * groups + group]
            at = lambda which: pltpu.roll(piece, (group - which) * span % LANES, 1)
            mine = lane_group == group
            rate = jnp.where(mine, at(0), rate)
            residue = jnp.where(mine, at(1), residue)
            skip = jnp.where(mine, at(2), skip)
        rates[tile] = rate
        gains[tile] = residue * jnp.sqrt(2.0 * rate)
        skips[tile] = skip
        power = []
        for slot, tokens in enumerate((1, steps, 2 * steps, 4 * steps, 8 * steps, 16 * steps)):
            value = jnp.exp(-float(tokens) * rate)
            power.append(value)
            decays[slot, tile] = value
        signal = [gate_in[tile, step] for step in range(steps)]
        row_tokens = row.astype(F32) * float(steps)
        for mode in range(modes):
            decay = row_of(power[0], mode)
            state = signal[0]
            for step in range(1, steps):
                state = decay * state + signal[step]
            for slot in range(3):
                reach = 1 << slot
                factor = jnp.where(row >= reach, row_of(power[1 + slot], mode), 0.0)
                state = state + factor * pltpu.roll(state, reach, 0)
            ends[tile, mode : mode + 1, :] = state[ROWS - 1 :, :]
            entry[tile, mode] = jnp.where(row >= 1, pltpu.roll(state, 1, 0), 0.0)
            entry_decay[tile, mode] = jnp.exp(-row_tokens * row_of(rate, mode))
        return carry

    lax.fori_loop(0, tiles, local_states, 0)

    pair = remote(ends, ends_other, pair_sem.at[0], pair_sem.at[1], {"ctx": partner})
    pair.start()
    pair.wait_recv()
    half = pl.ds(core * half_tiles, half_tiles)
    mine, other = ends[half], ends_other[half]
    first = jnp.where(core == 0, mine, other)
    second = jnp.where(core == 0, other, mine)
    chip_end[...] = decays[4, half] * first + second
    n_chips = n_ctx // 2

    def chip_copy(source, target):
        return remote(
            chip_end, chip_ends.at[source], chip_send.at[target], chip_recv.at[source], {"ctx": 2 * target + core}
        )

    def send_chip(target, carry):
        chip_copy(chip, target).start()
        return carry

    lax.fori_loop(chip + 1, n_chips, send_chip, 0)
    long_decay = decays[5, half]

    def take_chip(source, total):
        chip_copy(source, source).wait_recv()
        return total * long_decay + chip_ends[source]

    carried[half] = lax.fori_loop(0, chip, take_chip, jnp.zeros(chip_end.shape, F32))
    give = remote(carried.at[half], carried.at[half], pair_sem.at[2], pair_sem.at[3], {"ctx": partner})
    give.start()
    other_half = pl.ds((1 - core) * half_tiles, half_tiles)
    remote(carried.at[half], carried.at[other_half], pair_sem.at[2], pair_sem.at[3], {"ctx": partner}).wait_recv()

    def long_conv(tile, carry):
        into_chip = carried[tile]
        into = jnp.where(core == 0, into_chip, decays[4, tile] * into_chip + ends_other[tile])
        power, gain = decays[0, tile], gains[tile]
        decay = [row_of(power, m) for m in range(modes)]
        weigh = [row_of(gain, m) for m in range(modes)]
        skip = row_of(skips[tile], 0)
        state = [entry[tile, m] + entry_decay[tile, m] * row_of(into, m) for m in range(modes)]
        for step in range(steps):
            signal = gate_in[tile, step]
            total = skip * signal
            for m in range(modes):
                state[m] = decay[m] * state[m] + signal
                total = total + weigh[m] * state[m]
            long_out = total.astype(BF16).astype(F32)
            gated_plain[pl.ds(step, ROWS, stride=steps), :] = query[tile, step] * long_out
        lanes = pl.ds(pl.multiple_of(tile * LANES, LANES), LANES)
        gated[own, :, lanes] = gated_plain[...].astype(BF16)
        return carry

    lax.fori_loop(0, tiles, long_conv, 0)

    def ring_device(to_z):
        return {"ctx": x_hi * per_x + 2 * to_z + core}

    devices = [ring_device(lax.rem(z + 1, nz)), ring_device(lax.rem(z + nz - 1, nz))]
    far = nz // 2
    half_rows = feats.shape[1] // 2

    def ring_halves(way, step):
        return [way, 1 - way] if step < far else [way]

    def ring_block(way, step):
        return 2 * lax.rem(z + (nz - step if way == 0 else step), nz) + core

    def ring_copy(block, way, step, part):
        rows = pl.ds(part * half_rows, half_rows)
        return remote(
            gated.at[block, rows],
            gated.at[block, rows],
            ring_send.at[way, step, part],
            gated_recv.at[block, part],
            devices[way],
        )

    def across_copy(block, slot):
        return remote(
            gated.at[block], gated.at[block], across_send.at[slot], gated_recv.at[block, 0], {"ctx": partner}
        )

    def cross_copy(block):
        return remote(
            crossing.at[block],
            crossed.at[block],
            cross_send.at[block],
            cross_recv.at[block],
            {"tp": (1 - x_lo) * ny + y},
        )

    def strip_copy(block, source, target):
        rows = pl.ds(pl.multiple_of(target * strip_rows, strip_rows), strip_rows)
        return remote(
            summed.at[block, rows],
            strips.at[source, block],
            strip_send.at[block, target],
            strip_recv.at[source, block],
            {"tp": x_lo * ny + target},
        )

    def piece_copy(block, which, strip):
        rows = pl.ds(pl.multiple_of(strip * strip_rows, strip_rows), strip_rows)
        return remote(
            mixed.at[block],
            pieces.at[which, rows],
            piece_send.at[block],
            piece_recv.at[which, strip],
            {"ctx": x_hi * per_x + block, "tp": x_lo * ny + final_y},
        )

    def stays(block):
        return jnp.logical_and(block == own, final_y == y)

    def multiply(block):
        value = jnp.dot(gated[block], weights[1 - x_lo], preferred_element_type=F32)
        crossing[block] = value.astype(BF16)
        cross_copy(block).start()
        kept[block] = jnp.dot(gated[block], weights[x_lo], preferred_element_type=F32)

    def combine(block):
        cross_copy(block).wait_recv()
        summed[block] = (kept[block] + crossed[block].astype(F32)).astype(BF16)
        for step in range(1, ny):
            strip_copy(block, y, lax.rem(y + step, ny)).start()

    def finish(block):
        own_rows = pl.ds(pl.multiple_of(y * strip_rows, strip_rows), strip_rows)
        total = summed[block, own_rows].astype(F32)
        for step in range(1, ny):
            source = lax.rem(y + step, ny)
            strip_copy(block, source, y).wait_recv()
            total = total + strips[source, block].astype(F32)
        value = total.astype(BF16)

        @pl.when(stays(block))
        def _():
            pieces[quarter, own_rows] = value

        @pl.when(jnp.logical_not(stays(block)))
        def _():
            mixed[block] = value
            piece_copy(block, quarter, y).start()

    for way in range(2):
        for part in ring_halves(way, 1):
            ring_copy(own, way, 0, part).start()
    across_copy(own, 0).start()
    weight_copy(1 - x_hi).wait_recv()

    done = []

    def advance(entry):
        block, waits = entry
        if waits:
            across_copy(block, 0).wait_recv()
        multiply(block)
        done.append(block)
        if len(done) > CROSS_LAG:
            combine(done[-1 - CROSS_LAG])
        if len(done) > STRIP_LAG:
            finish(done[-1 - STRIP_LAG])

    def other(block):
        return block + 1 - 2 * core

    pending = [(own, False)]
    later = [(other(own), True)]
    for step in range(1, far + 1):
        ways = [0, 1]
        arrived = [ring_block(way, step) for way in ways]
        for turn in range(len(ring_halves(0, step))):
            for way in ways:
                part = ring_halves(way, step)[turn]
                ring_copy(arrived[way], way, 0, part).wait_recv()
                if step < far and part in ring_halves(way, step + 1):
                    ring_copy(arrived[way], way, step, part).start()
            if turn == 0:
                for _ in range(min(2, len(pending))):
                    advance(pending.pop(0))
        blocks = arrived if step < far else arrived[:1]
        for index, block in enumerate(blocks):
            across_copy(block, 2 * step - 1 + index).start()
        while pending:
            advance(pending.pop(0))
        pending = later + [(block, False) for block in blocks]
        later = [(other(block), True) for block in blocks]
    for entry_left in pending + later:
        advance(entry_left)
    total_blocks = len(done)
    for index in range(total_blocks - CROSS_LAG, total_blocks):
        combine(done[index])
    for index in range(total_blocks - STRIP_LAG, total_blocks):
        finish(done[index])

    cols = out.shape[1] // 4
    for which in range(4):
        for strip in range(ny):
            here = jnp.logical_and(jnp.logical_and(final_y == y, quarter == which), y == strip)

            @pl.when(jnp.logical_not(here))
            def _():
                piece_copy(own, which, strip).wait_recv()

        out[:, which * cols : (which + 1) * cols] = pieces[which]

    @pl.when(me < n_ctx - 1)
    def _():
        halo_copy(me + 1).wait_send()

    def drain_params(step, carry):
        param_copy(step, me, lax.rem(me + step, n_ctx)).wait_send()
        return carry

    lax.fori_loop(1, n_ctx, drain_params, 0)
    weight_copy(x_hi).wait_send()
    pair.wait_send()
    give.wait_send()

    def drain_chip(target, carry):
        chip_copy(chip, target).wait_send()
        return carry

    lax.fori_loop(chip + 1, n_chips, drain_chip, 0)
    for step in range(far):
        for way in range(2):
            for part in ring_halves(way, step + 1):
                ring_copy(own, way, step, part).wait_send()
    for slot in range(nz):
        across_copy(own, slot).wait_send()

    def drain_blocks(block, carry):
        cross_copy(block).wait_send()
        for step in range(1, ny):
            strip_copy(block, y, lax.rem(y + step, ny)).wait_send()

        @pl.when(jnp.logical_not(stays(block)))
        def _():
            piece_copy(block, quarter, y).wait_send()

        return carry

    lax.fori_loop(0, per_x, drain_blocks, 0)


def per_device(n_ctx, n_tp, features, conv_weight, decay_rates, residues, skip_gain, out_weight):
    nz, ny = n_ctx // 4, n_tp // 2
    _, rows, width = features.shape
    modes, span = decay_rates.shape
    tiles, steps = width // LANES, rows // ROWS
    cols = out_weight.shape[1]
    blocks = 2 * nz
    tile_state = (tiles, modes, LANES)
    row_state = (tiles, modes, ROWS, LANES)
    half_state = (tiles // 2, modes, LANES)
    dma = pltpu.SemaphoreType.DMA
    vmem = pl.BlockSpec(memory_space=pltpu.VMEM)
    return pl.pallas_call(
        functools.partial(kernel, (nz, ny, n_ctx, n_tp)),
        out_shape=jax.ShapeDtypeStruct((rows, 4 * cols), BF16),
        in_specs=[pl.BlockSpec(memory_space=pltpu.HBM)] * 6,
        out_specs=vmem,
        scratch_shapes=[
            pltpu.VMEM(features.shape, BF16),
            pltpu.VMEM(conv_weight.shape[:2] + (width,), F32),
            pltpu.VMEM((modes, span), F32),
            pltpu.VMEM((modes, span), F32),
            pltpu.VMEM((1, span), F32),
            pltpu.VMEM((modes, LANES), F32),
            pltpu.VMEM((n_ctx, modes, LANES), F32),
            pltpu.VMEM((3, 16, width), BF16),
            pltpu.VMEM((3, rows, LANES), F32),
            pltpu.VMEM((tiles, steps, ROWS, LANES), F32),
            pltpu.VMEM((tiles, steps, ROWS, LANES), F32),
            pltpu.VMEM(tile_state, F32),
            pltpu.VMEM(tile_state, F32),
            pltpu.VMEM(tile_state, F32),
            pltpu.VMEM((DECAY_STEPS,) + tile_state, F32),
            pltpu.VMEM(tile_state, F32),
            pltpu.VMEM(tile_state, F32),
            pltpu.VMEM(half_state, F32),
            pltpu.VMEM((n_ctx // 2,) + half_state, F32),
            pltpu.VMEM(tile_state, F32),
            pltpu.VMEM(row_state, F32),
            pltpu.VMEM(row_state, F32),
            pltpu.VMEM((rows, LANES), F32),
            pltpu.VMEM((blocks, rows, width), BF16),
            pltpu.VMEM((2, width, cols), BF16),
            pltpu.VMEM((blocks, rows, cols), F32),
            pltpu.VMEM((blocks, rows, cols), BF16),
            pltpu.VMEM((blocks, rows, cols), BF16),
            pltpu.VMEM((blocks, rows, cols), BF16),
            pltpu.VMEM((ny, blocks, rows // ny, cols), BF16),
            pltpu.VMEM((blocks, rows // ny, cols), BF16),
            pltpu.VMEM((4, rows, cols), BF16),
            dma((6,)),
            dma((2,)),
            dma((2,)),
            dma((4,)),
            dma((n_ctx,)),
            dma((n_ctx,)),
            dma((n_ctx // 2,)),
            dma((n_ctx // 2,)),
            dma((2, nz // 2, 2)),
            dma((nz,)),
            dma((blocks, 2)),
            dma((blocks,)),
            dma((blocks,)),
            dma((blocks, ny)),
            dma((ny, blocks)),
            dma((blocks,)),
            dma((4, ny)),
        ],
        compiler_params=pltpu.CompilerParams(
            collective_id=0, has_side_effects=True, vmem_limit_bytes=67_000_000
        ),
    )(features, conv_weight, decay_rates, residues, skip_gain[None, :], out_weight)


def solution(mesh):
    in_specs = (
        P(None, "ctx", "tp"),
        P(),
        P(None, ("tp", "ctx")),
        P(None, ("tp", "ctx")),
        P(("tp", "ctx")),
        P("tp", "ctx"),
    )
    return jax.shard_map(
        functools.partial(per_device, mesh.shape["ctx"], mesh.shape["tp"]),
        mesh=mesh,
        in_specs=in_specs,
        out_specs=P("ctx", "tp"),
        check_vma=False,
    )
```

```python
import functools

import jax
import jax.numpy as jnp
from jax import lax
from jax.experimental import pallas as pl
from jax.experimental.pallas import tpu as pltpu
from jax.sharding import PartitionSpec as P

MESH = pl.DeviceIdType.MESH
F32 = jnp.float32
BF16 = jnp.bfloat16
LANES = 128
ROWS = 8
CROSS_LAG = 3
STRIP_LAG = 6
DECAY_STEPS = 6


def row_of(tile, index):
    return jnp.broadcast_to(tile[index : index + 1, :], (ROWS, LANES))


def kernel(
    dims,
    features,
    all_taps,
    decay_rates,
    residues,
    skip_gain,
    weight,
    out,
    feats,
    conv_weight,
    own_rates,
    own_residues,
    own_skip,
    pack,
    params,
    halo,
    plain,
    gate_in,
    query,
    rates,
    gains,
    skips,
    decays,
    ends,
    ends_other,
    chip_end,
    chip_ends,
    plane_total,
    carried,
    entry,
    entry_decay,
    gated_plain,
    gated,
    weights,
    kept,
    crossing,
    crossed,
    summed,
    strips,
    mixed,
    pieces,
    fetch_sem,
    halo_sem,
    weight_sem,
    pair_sem,
    param_send,
    param_recv,
    chip_send,
    chip_recv,
    plane_sem,
    ring_send,
    across_send,
    gated_recv,
    cross_send,
    cross_recv,
    strip_send,
    strip_recv,
    piece_send,
    piece_recv,
):
    nz, ny, n_ctx, n_tp = dims
    per_x = 2 * nz
    modes = rates.shape[1]
    tiles = feats.shape[2] // LANES
    half_tiles = tiles // 2
    steps = feats.shape[1] // ROWS
    width = feats.shape[2]
    me = lax.axis_index("ctx")
    tp = lax.axis_index("tp")
    core = lax.rem(me, 2)
    chip = lax.div(me, 2)
    x_hi = lax.div(me, per_x)
    z = lax.rem(chip, nz)
    x_lo = lax.div(tp, ny)
    y = lax.rem(tp, ny)
    own = lax.rem(me, per_x)
    partner = me + 1 - 2 * core
    x_partner = lax.rem(me + per_x, n_ctx)
    final_y = lax.div(z, 2)
    quarter = lax.rem(me, 4)
    strip_rows = feats.shape[1] // ny

    def remote(src, dst, send, recv, device):
        return pltpu.make_async_remote_copy(
            src_ref=src, dst_ref=dst, send_sem=send, recv_sem=recv, device_id=device, device_id_type=MESH
        )

    own_lanes = pl.ds(pl.multiple_of(tp * width, width), width)
    fetches = [
        pltpu.make_async_copy(src, dst, fetch_sem.at[slot])
        for slot, (src, dst) in enumerate(
            [
                (decay_rates, own_rates),
                (residues, own_residues),
                (skip_gain, own_skip),
                (features, feats),
                (all_taps.at[:, :, own_lanes], conv_weight),
                (weight, weights.at[x_hi]),
            ]
        )
    ]
    for fetch in fetches:
        fetch.start()

    barrier = pltpu.get_barrier_semaphore()

    def greet_ctx(step, carry):
        pl.semaphore_signal(barrier, inc=1, device_id={"ctx": lax.rem(me + step, n_ctx)}, device_id_type=MESH)
        return carry

    def greet_tp(step, carry):
        pl.semaphore_signal(barrier, inc=1, device_id={"tp": lax.rem(tp + step, n_tp)}, device_id_type=MESH)
        return carry

    lax.fori_loop(1, n_ctx, greet_ctx, 0)
    lax.fori_loop(1, n_tp, greet_tp, 0)
    for other_y in range(1, ny):
        for which in range(4):
            pl.semaphore_signal(
                barrier,
                inc=1,
                device_id={"ctx": x_hi * per_x + 4 * y + which, "tp": x_lo * ny + lax.rem(y + other_y, ny)},
                device_id_type=MESH,
            )

    for fetch in fetches:
        fetch.wait()
    modes_shape = own_rates.shape
    packed = jnp.concatenate(
        [
            own_rates[...],
            own_residues[...],
            jnp.broadcast_to(own_skip[...], modes_shape),
            jnp.zeros((modes_shape[0], LANES - 3 * modes_shape[1]), F32),
        ],
        axis=1,
    )
    pack[...] = packed
    params[me] = packed

    pl.semaphore_wait(barrier, n_ctx + n_tp - 2 + jnp.where(final_y != y, per_x, 0))

    last_rows = pl.ds(feats.shape[1] - halo.shape[1], halo.shape[1])

    def halo_copy(device):
        return remote(feats.at[:, last_rows, :], halo, halo_sem.at[0], halo_sem.at[1], {"ctx": device})

    def param_copy(step, source, device):
        return remote(pack, params.at[source], param_send.at[step], param_recv.at[source], {"ctx": device})

    def weight_copy(slot):
        return remote(weights.at[slot], weights.at[slot], weight_sem.at[0], weight_sem.at[1], {"ctx": x_partner})

    @pl.when(me < n_ctx - 1)
    def _():
        halo_copy(me + 1).start()

    n_chips = n_ctx // 2

    def chip_at(step):
        return 2 * lax.rem(chip + step, n_chips) + core

    def send_params(step, carry):
        param_copy(step, me, chip_at(step)).start()
        return carry

    own_across = remote(pack, params.at[me], param_send.at[0], param_recv.at[me], {"ctx": partner})
    own_across.start()
    lax.fori_loop(1, n_chips, send_params, 0)
    weight_copy(x_hi).start()

    @pl.when(me > 0)
    def _():
        halo_copy(me - 1).wait_recv()

    @pl.when(me == 0)
    def _():
        halo[...] = jnp.zeros_like(halo)

    row = lax.broadcasted_iota(jnp.int32, (ROWS, LANES), 0)
    lane_group = lax.broadcasted_iota(jnp.int32, (modes, LANES), 1) // (width // n_ctx)
    groups = LANES * n_ctx // width

    def short_conv(tile, carry):
        lanes = pl.ds(pl.multiple_of(tile * LANES, LANES), LANES)
        filtered = []
        for kind in range(3):
            plain[kind] = feats[kind, :, lanes].astype(F32)
            before = halo[kind, :, lanes].astype(F32)
            taps = conv_weight[kind, :, lanes]
            tap = [row_of(taps, j) for j in range(3)]
            now = [plain[kind, pl.ds(step, ROWS, stride=steps), :] for step in range(steps)]
            last = halo.shape[1] - 1
            one = jnp.where(row == 0, row_of(before, last), pltpu.roll(now[steps - 1], 1, 0))
            two = jnp.where(row == 0, row_of(before, last - 1), pltpu.roll(now[steps - 2], 1, 0))
            chain = [two, one] + now
            filtered.append(
                [tap[0] * chain[s + 2] + tap[1] * chain[s + 1] + tap[2] * chain[s] for s in range(steps)]
            )
        for step in range(steps):
            query[tile, step] = filtered[0][step]
            gate_in[tile, step] = (filtered[1][step] * filtered[2][step]).astype(BF16).astype(F32)
        return carry

    lax.fori_loop(0, tiles, short_conv, 0)

    def relay_copy(step, source):
        return remote(
            params.at[source],
            params.at[source],
            param_send.at[n_chips + step],
            param_recv.at[source],
            {"ctx": partner},
        )

    def relay_params(step, carry):
        source = chip_at(step)
        param_copy(step, source, source).wait_recv()
        relay_copy(step, source).start()
        return carry

    lax.fori_loop(1, n_chips, relay_params, 0)

    def wait_params(step, carry):
        relay_copy(0, chip_at(step) + 1 - 2 * core).wait_recv()
        return carry

    lax.fori_loop(0, n_chips, wait_params, 0)

    span = width // n_ctx

    def local_states(tile, carry):
        rate = jnp.zeros((modes, LANES), F32)
        residue = jnp.zeros((modes, LANES), F32)
        skip = jnp.zeros((modes, LANES), F32)
        for group in range(groups):
            piece = params[tile * groups + group]
            at = lambda which: pltpu.roll(piece, (group - which) * span % LANES, 1)
            mine = lane_group == group
            rate = jnp.where(mine, at(0), rate)
            residue = jnp.where(mine, at(1), residue)
            skip = jnp.where(mine, at(2), skip)
        rates[tile] = rate
        gains[tile] = residue * jnp.sqrt(2.0 * rate)
        skips[tile] = skip
        power = []
        for slot, tokens in enumerate((1, steps, 2 * steps, 4 * steps, 8 * steps, 16 * steps)):
            value = jnp.exp(-float(tokens) * rate)
            power.append(value)
            decays[slot, tile] = value
        signal = [gate_in[tile, step] for step in range(steps)]
        row_tokens = row.astype(F32) * float(steps)
        for mode in range(modes):
            decay = row_of(power[0], mode)
            state = signal[0]
            for step in range(1, steps):
                state = decay * state + signal[step]
            for slot in range(3):
                reach = 1 << slot
                factor = jnp.where(row >= reach, row_of(power[1 + slot], mode), 0.0)
                state = state + factor * pltpu.roll(state, reach, 0)
            ends[tile, mode : mode + 1, :] = state[ROWS - 1 :, :]
            entry[tile, mode] = jnp.where(row >= 1, pltpu.roll(state, 1, 0), 0.0)
            entry_decay[tile, mode] = jnp.exp(-row_tokens * row_of(rate, mode))
        return carry

    lax.fori_loop(0, tiles, local_states, 0)

    pair = remote(ends, ends_other, pair_sem.at[0], pair_sem.at[1], {"ctx": partner})
    pair.start()
    pair.wait_recv()
    half = pl.ds(core * half_tiles, half_tiles)
    mine, other = ends[half], ends_other[half]
    first = jnp.where(core == 0, mine, other)
    second = jnp.where(core == 0, other, mine)
    chip_end[...] = decays[4, half] * first + second

    def chip_copy(source, target):
        return remote(
            chip_end, chip_ends.at[source], chip_send.at[target], chip_recv.at[source], {"ctx": 2 * target + core}
        )

    def each_target(act):
        def body(step, carry):
            to_z = lax.rem(z + step, nz)

            @pl.when(jnp.logical_or(x_hi == 0, to_z > z))
            def _():
                act(chip_copy(chip, x_hi * nz + to_z))

            return carry

        lax.fori_loop(1, nz, body, 0)

    each_target(lambda copy: copy.start())
    long_decay = decays[5, half]
    total_copy = remote(plane_total, plane_total, plane_sem.at[0], plane_sem.at[1], {"ctx": x_partner})

    def take_chip(source, state):
        total, power = state
        chip_copy(source, source).wait_recv()
        return total * long_decay + chip_ends[source], power * long_decay

    nothing = jnp.zeros(chip_end.shape, F32)
    before_here, reach_back = lax.fori_loop(x_hi * nz, chip, take_chip, (nothing, nothing + 1.0))
    carried[half] = before_here

    @pl.when(x_hi == 1)
    def _():
        total_copy.wait_recv()
        carried[half] = carried[half] + reach_back * plane_total[...]

    give = remote(carried.at[half], carried.at[half], pair_sem.at[2], pair_sem.at[3], {"ctx": partner})
    give.start()

    @pl.when(x_hi == 0)
    def _():
        through_here = before_here * long_decay + chip_end[...]
        whole, _ = lax.fori_loop(chip + 1, nz, take_chip, (through_here, nothing))
        plane_total[...] = whole
        total_copy.start()

    other_half = pl.ds((1 - core) * half_tiles, half_tiles)
    remote(carried.at[half], carried.at[other_half], pair_sem.at[2], pair_sem.at[3], {"ctx": partner}).wait_recv()

    def long_conv(tile, carry):
        into_chip = carried[tile]
        into = jnp.where(core == 0, into_chip, decays[4, tile] * into_chip + ends_other[tile])
        power, gain = decays[0, tile], gains[tile]
        decay = [row_of(power, m) for m in range(modes)]
        weigh = [row_of(gain, m) for m in range(modes)]
        skip = row_of(skips[tile], 0)
        state = [entry[tile, m] + entry_decay[tile, m] * row_of(into, m) for m in range(modes)]
        for step in range(steps):
            signal = gate_in[tile, step]
            total = skip * signal
            for m in range(modes):
                state[m] = decay[m] * state[m] + signal
                total = total + weigh[m] * state[m]
            long_out = total.astype(BF16).astype(F32)
            gated_plain[pl.ds(step, ROWS, stride=steps), :] = query[tile, step] * long_out
        lanes = pl.ds(pl.multiple_of(tile * LANES, LANES), LANES)
        gated[own, :, lanes] = gated_plain[...].astype(BF16)
        return carry

    lax.fori_loop(0, tiles, long_conv, 0)

    def ring_device(to_z):
        return {"ctx": x_hi * per_x + 2 * to_z + core}

    devices = [ring_device(lax.rem(z + 1, nz)), ring_device(lax.rem(z + nz - 1, nz))]
    far = nz // 2
    half_rows = feats.shape[1] // 2

    def ring_halves(way, step):
        return [way, 1 - way] if step < far else [way]

    def ring_block(way, step):
        return 2 * lax.rem(z + (nz - step if way == 0 else step), nz) + core

    def ring_copy(block, way, step, part):
        rows = pl.ds(part * half_rows, half_rows)
        return remote(
            gated.at[block, rows],
            gated.at[block, rows],
            ring_send.at[way, step, part],
            gated_recv.at[block, part],
            devices[way],
        )

    def across_copy(block, slot):
        return remote(
            gated.at[block], gated.at[block], across_send.at[slot], gated_recv.at[block, 0], {"ctx": partner}
        )

    def cross_copy(block):
        return remote(
            crossing.at[block],
            crossed.at[block],
            cross_send.at[block],
            cross_recv.at[block],
            {"tp": (1 - x_lo) * ny + y},
        )

    def strip_copy(block, source, target):
        rows = pl.ds(pl.multiple_of(target * strip_rows, strip_rows), strip_rows)
        return remote(
            summed.at[block, rows],
            strips.at[source, block],
            strip_send.at[block, target],
            strip_recv.at[source, block],
            {"tp": x_lo * ny + target},
        )

    def piece_copy(block, which, strip):
        rows = pl.ds(pl.multiple_of(strip * strip_rows, strip_rows), strip_rows)
        return remote(
            mixed.at[block],
            pieces.at[which, rows],
            piece_send.at[block],
            piece_recv.at[which, strip],
            {"ctx": x_hi * per_x + block, "tp": x_lo * ny + final_y},
        )

    def stays(block):
        return jnp.logical_and(block == own, final_y == y)

    def multiply(block):
        value = jnp.dot(gated[block], weights[1 - x_lo], preferred_element_type=F32)
        crossing[block] = value.astype(BF16)
        cross_copy(block).start()
        kept[block] = jnp.dot(gated[block], weights[x_lo], preferred_element_type=F32)

    def combine(block):
        cross_copy(block).wait_recv()
        summed[block] = (kept[block] + crossed[block].astype(F32)).astype(BF16)
        for step in range(1, ny):
            strip_copy(block, y, lax.rem(y + step, ny)).start()

    def finish(block):
        own_rows = pl.ds(pl.multiple_of(y * strip_rows, strip_rows), strip_rows)
        total = summed[block, own_rows].astype(F32)
        for step in range(1, ny):
            source = lax.rem(y + step, ny)
            strip_copy(block, source, y).wait_recv()
            total = total + strips[source, block].astype(F32)
        value = total.astype(BF16)

        @pl.when(stays(block))
        def _():
            pieces[quarter, own_rows] = value

        @pl.when(jnp.logical_not(stays(block)))
        def _():
            mixed[block] = value
            piece_copy(block, quarter, y).start()

    for way in range(2):
        for part in ring_halves(way, 1):
            ring_copy(own, way, 0, part).start()
    across_copy(own, 0).start()
    weight_copy(1 - x_hi).wait_recv()

    done = []

    def advance(entry):
        block, waits = entry
        if waits:
            across_copy(block, 0).wait_recv()
        multiply(block)
        done.append(block)
        if len(done) > CROSS_LAG:
            combine(done[-1 - CROSS_LAG])
        if len(done) > STRIP_LAG:
            finish(done[-1 - STRIP_LAG])

    def other(block):
        return block + 1 - 2 * core

    pending = [(own, False)]
    later = [(other(own), True)]
    for step in range(1, far + 1):
        ways = [0, 1]
        arrived = [ring_block(way, step) for way in ways]
        for turn in range(len(ring_halves(0, step))):
            for way in ways:
                part = ring_halves(way, step)[turn]
                ring_copy(arrived[way], way, 0, part).wait_recv()
                if step < far and part in ring_halves(way, step + 1):
                    ring_copy(arrived[way], way, step, part).start()
            if turn == 0:
                for _ in range(min(2, len(pending))):
                    advance(pending.pop(0))
        blocks = arrived if step < far else arrived[:1]
        for index, block in enumerate(blocks):
            across_copy(block, 2 * step - 1 + index).start()
        while pending:
            advance(pending.pop(0))
        pending = later + [(block, False) for block in blocks]
        later = [(other(block), True) for block in blocks]
    for entry_left in pending + later:
        advance(entry_left)
    total_blocks = len(done)
    for index in range(total_blocks - CROSS_LAG, total_blocks):
        combine(done[index])
    for index in range(total_blocks - STRIP_LAG, total_blocks):
        finish(done[index])

    cols = out.shape[1] // 4
    for which in range(4):
        for strip in range(ny):
            here = jnp.logical_and(jnp.logical_and(final_y == y, quarter == which), y == strip)

            @pl.when(jnp.logical_not(here))
            def _():
                piece_copy(own, which, strip).wait_recv()

        out[:, which * cols : (which + 1) * cols] = pieces[which]

    @pl.when(me < n_ctx - 1)
    def _():
        halo_copy(me + 1).wait_send()

    def drain_params(step, carry):
        param_copy(step, me, chip_at(step)).wait_send()
        relay_copy(step, chip_at(step)).wait_send()
        return carry

    own_across.wait_send()
    lax.fori_loop(1, n_chips, drain_params, 0)
    weight_copy(x_hi).wait_send()
    pair.wait_send()
    give.wait_send()

    each_target(lambda copy: copy.wait_send())

    @pl.when(x_hi == 0)
    def _():
        total_copy.wait_send()

    for step in range(far):
        for way in range(2):
            for part in ring_halves(way, step + 1):
                ring_copy(own, way, step, part).wait_send()
    for slot in range(nz):
        across_copy(own, slot).wait_send()

    def drain_blocks(block, carry):
        cross_copy(block).wait_send()
        for step in range(1, ny):
            strip_copy(block, y, lax.rem(y + step, ny)).wait_send()

        @pl.when(jnp.logical_not(stays(block)))
        def _():
            piece_copy(block, quarter, y).wait_send()

        return carry

    lax.fori_loop(0, per_x, drain_blocks, 0)


def per_device(n_ctx, n_tp, features, conv_weight, decay_rates, residues, skip_gain, out_weight):
    nz, ny = n_ctx // 4, n_tp // 2
    _, rows, width = features.shape
    modes, span = decay_rates.shape
    tiles, steps = width // LANES, rows // ROWS
    cols = out_weight.shape[1]
    blocks = 2 * nz
    tile_state = (tiles, modes, LANES)
    row_state = (tiles, modes, ROWS, LANES)
    half_state = (tiles // 2, modes, LANES)
    dma = pltpu.SemaphoreType.DMA
    vmem = pl.BlockSpec(memory_space=pltpu.VMEM)
    return pl.pallas_call(
        functools.partial(kernel, (nz, ny, n_ctx, n_tp)),
        out_shape=jax.ShapeDtypeStruct((rows, 4 * cols), BF16),
        in_specs=[pl.BlockSpec(memory_space=pltpu.HBM)] * 6,
        out_specs=vmem,
        scratch_shapes=[
            pltpu.VMEM(features.shape, BF16),
            pltpu.VMEM(conv_weight.shape[:2] + (width,), F32),
            pltpu.VMEM((modes, span), F32),
            pltpu.VMEM((modes, span), F32),
            pltpu.VMEM((1, span), F32),
            pltpu.VMEM((modes, LANES), F32),
            pltpu.VMEM((n_ctx, modes, LANES), F32),
            pltpu.VMEM((3, 16, width), BF16),
            pltpu.VMEM((3, rows, LANES), F32),
            pltpu.VMEM((tiles, steps, ROWS, LANES), F32),
            pltpu.VMEM((tiles, steps, ROWS, LANES), F32),
            pltpu.VMEM(tile_state, F32),
            pltpu.VMEM(tile_state, F32),
            pltpu.VMEM(tile_state, F32),
            pltpu.VMEM((DECAY_STEPS,) + tile_state, F32),
            pltpu.VMEM(tile_state, F32),
            pltpu.VMEM(tile_state, F32),
            pltpu.VMEM(half_state, F32),
            pltpu.VMEM((n_ctx // 2,) + half_state, F32),
            pltpu.VMEM(half_state, F32),
            pltpu.VMEM(tile_state, F32),
            pltpu.VMEM(row_state, F32),
            pltpu.VMEM(row_state, F32),
            pltpu.VMEM((rows, LANES), F32),
            pltpu.VMEM((blocks, rows, width), BF16),
            pltpu.VMEM((2, width, cols), BF16),
            pltpu.VMEM((blocks, rows, cols), F32),
            pltpu.VMEM((blocks, rows, cols), BF16),
            pltpu.VMEM((blocks, rows, cols), BF16),
            pltpu.VMEM((blocks, rows, cols), BF16),
            pltpu.VMEM((ny, blocks, rows // ny, cols), BF16),
            pltpu.VMEM((blocks, rows // ny, cols), BF16),
            pltpu.VMEM((4, rows, cols), BF16),
            dma((6,)),
            dma((2,)),
            dma((2,)),
            dma((4,)),
            dma((n_ctx,)),
            dma((n_ctx,)),
            dma((n_ctx // 2,)),
            dma((n_ctx // 2,)),
            dma((2,)),
            dma((2, nz // 2, 2)),
            dma((nz,)),
            dma((blocks, 2)),
            dma((blocks,)),
            dma((blocks,)),
            dma((blocks, ny)),
            dma((ny, blocks)),
            dma((blocks,)),
            dma((4, ny)),
        ],
        compiler_params=pltpu.CompilerParams(
            collective_id=0, has_side_effects=True, vmem_limit_bytes=67_000_000
        ),
    )(features, conv_weight, decay_rates, residues, skip_gain[None, :], out_weight)


def solution(mesh):
    in_specs = (
        P(None, "ctx", "tp"),
        P(),
        P(None, ("tp", "ctx")),
        P(None, ("tp", "ctx")),
        P(("tp", "ctx")),
        P("tp", "ctx"),
    )
    return jax.shard_map(
        functools.partial(per_device, mesh.shape["ctx"], mesh.shape["tp"]),
        mesh=mesh,
        in_specs=in_specs,
        out_specs=P("ctx", "tp"),
        check_vma=False,
    )
```

```python
import functools

import jax
import jax.numpy as jnp
from jax import lax
from jax.experimental import pallas as pl
from jax.experimental.pallas import tpu as pltpu
from jax.sharding import PartitionSpec as P

MESH = pl.DeviceIdType.MESH
F32 = jnp.float32
BF16 = jnp.bfloat16
LANES = 128
ROWS = 8
CROSS_LAG = 3
STRIP_LAG = 6
DECAY_STEPS = 6


def row_of(tile, index):
    return jnp.broadcast_to(tile[index : index + 1, :], (ROWS, LANES))


def kernel(
    dims,
    features,
    all_taps,
    decay_rates,
    residues,
    skip_gain,
    weight,
    out,
    feats,
    conv_weight,
    own_rates,
    own_residues,
    own_skip,
    pack,
    params,
    halo,
    plain,
    gate_in,
    query,
    rates,
    gains,
    skips,
    decays,
    ends,
    ends_other,
    chip_end,
    chip_ends,
    plane_total,
    carried,
    entry,
    entry_decay,
    gated_plain,
    gated,
    weights,
    kept,
    crossing,
    crossed,
    summed,
    strips,
    mixed,
    pieces,
    fetch_sem,
    halo_sem,
    weight_sem,
    pair_sem,
    param_send,
    param_recv,
    chip_send,
    chip_recv,
    plane_sem,
    ring_send,
    across_send,
    gated_recv,
    cross_send,
    cross_recv,
    strip_send,
    strip_recv,
    piece_send,
    piece_recv,
):
    nz, ny, n_ctx, n_tp = dims
    per_x = 2 * nz
    modes = rates.shape[1]
    tiles = feats.shape[2] // LANES
    half_tiles = tiles // 2
    steps = feats.shape[1] // ROWS
    width = feats.shape[2]
    me = lax.axis_index("ctx")
    tp = lax.axis_index("tp")
    core = lax.rem(me, 2)
    chip = lax.div(me, 2)
    x_hi = lax.div(me, per_x)
    z = lax.rem(chip, nz)
    x_lo = lax.div(tp, ny)
    y = lax.rem(tp, ny)
    own = lax.rem(me, per_x)
    partner = me + 1 - 2 * core
    x_partner = lax.rem(me + per_x, n_ctx)
    final_y = lax.div(z, 2)
    quarter = lax.rem(me, 4)
    strip_rows = feats.shape[1] // ny

    def remote(src, dst, send, recv, device):
        return pltpu.make_async_remote_copy(
            src_ref=src, dst_ref=dst, send_sem=send, recv_sem=recv, device_id=device, device_id_type=MESH
        )

    own_lanes = pl.ds(pl.multiple_of(tp * width, width), width)
    fetches = [
        pltpu.make_async_copy(src, dst, fetch_sem.at[slot])
        for slot, (src, dst) in enumerate(
            [
                (decay_rates, own_rates),
                (residues, own_residues),
                (skip_gain, own_skip),
                (features, feats),
                (all_taps.at[:, :, own_lanes], conv_weight),
                (weight, weights.at[x_hi]),
            ]
        )
    ]
    for fetch in fetches:
        fetch.start()

    barrier = pltpu.get_barrier_semaphore()

    def greet_ctx(step, carry):
        pl.semaphore_signal(barrier, inc=1, device_id={"ctx": lax.rem(me + step, n_ctx)}, device_id_type=MESH)
        return carry

    def greet_tp(step, carry):
        pl.semaphore_signal(barrier, inc=1, device_id={"tp": lax.rem(tp + step, n_tp)}, device_id_type=MESH)
        return carry

    lax.fori_loop(1, n_ctx, greet_ctx, 0)
    lax.fori_loop(1, n_tp, greet_tp, 0)
    for other_y in range(1, ny):
        for which in range(4):
            pl.semaphore_signal(
                barrier,
                inc=1,
                device_id={"ctx": x_hi * per_x + 4 * y + which, "tp": x_lo * ny + lax.rem(y + other_y, ny)},
                device_id_type=MESH,
            )

    for fetch in fetches:
        fetch.wait()
    modes_shape = own_rates.shape
    packed = jnp.concatenate(
        [
            own_rates[...],
            own_residues[...],
            jnp.broadcast_to(own_skip[...], modes_shape),
            jnp.zeros((modes_shape[0], LANES - 3 * modes_shape[1]), F32),
        ],
        axis=1,
    )
    pack[...] = packed
    params[me] = packed

    pl.semaphore_wait(barrier, n_ctx + n_tp - 2 + jnp.where(final_y != y, per_x, 0))

    last_rows = pl.ds(feats.shape[1] - halo.shape[1], halo.shape[1])

    def halo_copy(device):
        return remote(feats.at[:, last_rows, :], halo, halo_sem.at[0], halo_sem.at[1], {"ctx": device})

    def param_copy(step, source, device):
        return remote(pack, params.at[source], param_send.at[step], param_recv.at[source], {"ctx": device})

    def weight_copy(slot):
        return remote(weights.at[slot], weights.at[slot], weight_sem.at[0], weight_sem.at[1], {"ctx": x_partner})

    @pl.when(me < n_ctx - 1)
    def _():
        halo_copy(me + 1).start()

    n_chips = n_ctx // 2

    def chip_at(step):
        return 2 * lax.rem(chip + step, n_chips) + core

    def send_params(step, carry):
        param_copy(step, me, chip_at(step)).start()
        return carry

    own_across = remote(pack, params.at[me], param_send.at[0], param_recv.at[me], {"ctx": partner})
    own_across.start()
    lax.fori_loop(1, n_chips, send_params, 0)
    weight_copy(x_hi).start()

    @pl.when(me > 0)
    def _():
        halo_copy(me - 1).wait_recv()

    @pl.when(me == 0)
    def _():
        halo[...] = jnp.zeros_like(halo)

    row = lax.broadcasted_iota(jnp.int32, (ROWS, LANES), 0)
    lane_group = lax.broadcasted_iota(jnp.int32, (modes, LANES), 1) // (width // n_ctx)
    groups = LANES * n_ctx // width

    def short_conv(tile, carry):
        lanes = pl.ds(pl.multiple_of(tile * LANES, LANES), LANES)
        filtered = []
        for kind in range(3):
            plain[kind] = feats[kind, :, lanes].astype(F32)
            before = halo[kind, :, lanes].astype(F32)
            taps = conv_weight[kind, :, lanes]
            tap = [row_of(taps, j) for j in range(3)]
            now = [plain[kind, pl.ds(step, ROWS, stride=steps), :] for step in range(steps)]
            last = halo.shape[1] - 1
            one = jnp.where(row == 0, row_of(before, last), pltpu.roll(now[steps - 1], 1, 0))
            two = jnp.where(row == 0, row_of(before, last - 1), pltpu.roll(now[steps - 2], 1, 0))
            chain = [two, one] + now
            filtered.append(
                [tap[0] * chain[s + 2] + tap[1] * chain[s + 1] + tap[2] * chain[s] for s in range(steps)]
            )
        for step in range(steps):
            query[tile, step] = filtered[0][step]
            gate_in[tile, step] = (filtered[1][step] * filtered[2][step]).astype(BF16).astype(F32)
        return carry

    lax.fori_loop(0, tiles, short_conv, 0)

    def relay_copy(step, source):
        return remote(
            params.at[source],
            params.at[source],
            param_send.at[n_chips + step],
            param_recv.at[source],
            {"ctx": partner},
        )

    def relay_params(step, carry):
        source = chip_at(step)
        param_copy(step, source, source).wait_recv()
        relay_copy(step, source).start()
        return carry

    lax.fori_loop(1, n_chips, relay_params, 0)

    def wait_params(step, carry):
        relay_copy(0, chip_at(step) + 1 - 2 * core).wait_recv()
        return carry

    lax.fori_loop(0, n_chips, wait_params, 0)

    span = width // n_ctx

    def local_states(tile, carry):
        rate = jnp.zeros((modes, LANES), F32)
        residue = jnp.zeros((modes, LANES), F32)
        skip = jnp.zeros((modes, LANES), F32)
        for group in range(groups):
            piece = params[tile * groups + group]
            at = lambda which: pltpu.roll(piece, (group - which) * span % LANES, 1)
            mine = lane_group == group
            rate = jnp.where(mine, at(0), rate)
            residue = jnp.where(mine, at(1), residue)
            skip = jnp.where(mine, at(2), skip)
        rates[tile] = rate
        gains[tile] = residue * jnp.sqrt(2.0 * rate)
        skips[tile] = skip
        power = []
        for slot, tokens in enumerate((1, steps, 2 * steps, 4 * steps, 8 * steps, 16 * steps)):
            value = jnp.exp(-float(tokens) * rate)
            power.append(value)
            decays[slot, tile] = value
        signal = [gate_in[tile, step] for step in range(steps)]
        row_tokens = row.astype(F32) * float(steps)
        for mode in range(modes):
            decay = row_of(power[0], mode)
            state = signal[0]
            for step in range(1, steps):
                state = decay * state + signal[step]
            for slot in range(3):
                reach = 1 << slot
                factor = jnp.where(row >= reach, row_of(power[1 + slot], mode), 0.0)
                state = state + factor * pltpu.roll(state, reach, 0)
            ends[tile, mode : mode + 1, :] = state[ROWS - 1 :, :]
            entry[tile, mode] = jnp.where(row >= 1, pltpu.roll(state, 1, 0), 0.0)
            entry_decay[tile, mode] = jnp.exp(-row_tokens * row_of(rate, mode))
        return carry

    lax.fori_loop(0, tiles, local_states, 0)

    pair = remote(ends, ends_other, pair_sem.at[0], pair_sem.at[1], {"ctx": partner})
    pair.start()
    pair.wait_recv()
    half = pl.ds(core * half_tiles, half_tiles)
    mine, other = ends[half], ends_other[half]
    first = jnp.where(core == 0, mine, other)
    second = jnp.where(core == 0, other, mine)
    chip_end[...] = decays[4, half] * first + second

    def chip_copy(source, target):
        return remote(
            chip_end, chip_ends.at[source], chip_send.at[target], chip_recv.at[source], {"ctx": 2 * target + core}
        )

    def each_target(act):
        def body(step, carry):
            to_z = lax.rem(z + step, nz)

            @pl.when(jnp.logical_or(x_hi == 0, to_z > z))
            def _():
                act(chip_copy(chip, x_hi * nz + to_z))

            return carry

        lax.fori_loop(1, nz, body, 0)

    each_target(lambda copy: copy.start())
    long_decay = decays[5, half]
    total_copy = remote(plane_total, plane_total, plane_sem.at[0], plane_sem.at[1], {"ctx": x_partner})

    def take_chip(source, state):
        total, power = state
        chip_copy(source, source).wait_recv()
        return total * long_decay + chip_ends[source], power * long_decay

    nothing = jnp.zeros(chip_end.shape, F32)
    before_here, reach_back = lax.fori_loop(x_hi * nz, chip, take_chip, (nothing, nothing + 1.0))
    carried[half] = before_here

    @pl.when(x_hi == 1)
    def _():
        total_copy.wait_recv()
        carried[half] = carried[half] + reach_back * plane_total[...]

    give = remote(carried.at[half], carried.at[half], pair_sem.at[2], pair_sem.at[3], {"ctx": partner})
    give.start()

    @pl.when(x_hi == 0)
    def _():
        through_here = before_here * long_decay + chip_end[...]
        whole, _ = lax.fori_loop(chip + 1, nz, take_chip, (through_here, nothing))
        plane_total[...] = whole
        total_copy.start()

    other_half = pl.ds((1 - core) * half_tiles, half_tiles)
    remote(carried.at[half], carried.at[other_half], pair_sem.at[2], pair_sem.at[3], {"ctx": partner}).wait_recv()

    def long_conv(tile, carry):
        into_chip = carried[tile]
        into = jnp.where(core == 0, into_chip, decays[4, tile] * into_chip + ends_other[tile])
        power, gain = decays[0, tile], gains[tile]
        decay = [row_of(power, m) for m in range(modes)]
        weigh = [row_of(gain, m) for m in range(modes)]
        skip = row_of(skips[tile], 0)
        state = [entry[tile, m] + entry_decay[tile, m] * row_of(into, m) for m in range(modes)]
        for step in range(steps):
            signal = gate_in[tile, step]
            total = skip * signal
            for m in range(modes):
                state[m] = decay[m] * state[m] + signal
                total = total + weigh[m] * state[m]
            long_out = total.astype(BF16).astype(F32)
            gated_plain[pl.ds(step, ROWS, stride=steps), :] = query[tile, step] * long_out
        lanes = pl.ds(pl.multiple_of(tile * LANES, LANES), LANES)
        gated[own, :, lanes] = gated_plain[...].astype(BF16)
        return carry

    lax.fori_loop(0, tiles, long_conv, 0)

    def ring_device(to_z):
        return {"ctx": x_hi * per_x + 2 * to_z + core}

    devices = [ring_device(lax.rem(z + 1, nz)), ring_device(lax.rem(z + nz - 1, nz))]
    far = nz // 2
    half_rows = feats.shape[1] // 2

    def ring_halves(way, step):
        return [way, 1 - way] if step < far else [way]

    def ring_block(way, step):
        return 2 * lax.rem(z + (nz - step if way == 0 else step), nz) + core

    def ring_copy(block, way, step, part):
        rows = pl.ds(part * half_rows, half_rows)
        return remote(
            gated.at[block, rows],
            gated.at[block, rows],
            ring_send.at[way, step, part],
            gated_recv.at[block, part],
            devices[way],
        )

    def across_copy(block, slot):
        return remote(
            gated.at[block], gated.at[block], across_send.at[slot], gated_recv.at[block, 0], {"ctx": partner}
        )

    def cross_copy(block):
        return remote(
            crossing.at[block],
            crossed.at[block],
            cross_send.at[block],
            cross_recv.at[block],
            {"tp": (1 - x_lo) * ny + y},
        )

    def strip_copy(block, source, target):
        rows = pl.ds(pl.multiple_of(target * strip_rows, strip_rows), strip_rows)
        return remote(
            summed.at[block, rows],
            strips.at[source, block],
            strip_send.at[block, target],
            strip_recv.at[source, block],
            {"tp": x_lo * ny + target},
        )

    def piece_copy(block, which, strip):
        rows = pl.ds(pl.multiple_of(strip * strip_rows, strip_rows), strip_rows)
        return remote(
            mixed.at[block],
            pieces.at[which, rows],
            piece_send.at[block],
            piece_recv.at[which, strip],
            {"ctx": x_hi * per_x + block, "tp": x_lo * ny + final_y},
        )

    def stays(block):
        return jnp.logical_and(block == own, final_y == y)

    def multiply(block):
        value = jnp.dot(gated[block], weights[1 - x_lo], preferred_element_type=F32)
        crossing[block] = value.astype(BF16)
        cross_copy(block).start()
        kept[block] = jnp.dot(gated[block], weights[x_lo], preferred_element_type=F32)

    def combine(block):
        cross_copy(block).wait_recv()
        summed[block] = (kept[block] + crossed[block].astype(F32)).astype(BF16)
        for step in range(1, ny):
            strip_copy(block, y, lax.rem(y + step, ny)).start()

    def finish(block):
        own_rows = pl.ds(pl.multiple_of(y * strip_rows, strip_rows), strip_rows)
        total = summed[block, own_rows].astype(F32)
        for step in range(1, ny):
            source = lax.rem(y + step, ny)
            strip_copy(block, source, y).wait_recv()
            total = total + strips[source, block].astype(F32)
        value = total.astype(BF16)

        @pl.when(stays(block))
        def _():
            pieces[quarter, own_rows] = value

        @pl.when(jnp.logical_not(stays(block)))
        def _():
            mixed[block] = value
            piece_copy(block, quarter, y).start()

    for way in range(2):
        for part in ring_halves(way, 1):
            ring_copy(own, way, 0, part).start()
    across_copy(own, 0).start()
    weight_copy(1 - x_hi).wait_recv()

    done = []

    def advance(entry):
        block, waits = entry
        if waits:
            across_copy(block, 0).wait_recv()
        multiply(block)
        done.append(block)
        if len(done) > CROSS_LAG:
            combine(done[-1 - CROSS_LAG])
        if len(done) > STRIP_LAG:
            finish(done[-1 - STRIP_LAG])

    def other(block):
        return block + 1 - 2 * core

    pending = [(own, False)]
    later = [(other(own), True)]
    for step in range(1, far + 1):
        ways = [0, 1]
        arrived = [ring_block(way, step) for way in ways]
        if step == far:
            for waiting in pending + later:
                advance(waiting)
            pending, later = [], []
        for turn in range(len(ring_halves(0, step))):
            for way in ways:
                part = ring_halves(way, step)[turn]
                ring_copy(arrived[way], way, 0, part).wait_recv()
                if step < far and part in ring_halves(way, step + 1):
                    ring_copy(arrived[way], way, step, part).start()
            if turn == 0:
                for _ in range(min(2, len(pending))):
                    advance(pending.pop(0))
        blocks = arrived if step < far else arrived[:1]
        for index, block in enumerate(blocks):
            across_copy(block, 2 * step - 1 + index).start()
        while pending:
            advance(pending.pop(0))
        pending = later + [(block, False) for block in blocks]
        later = [(other(block), True) for block in blocks]
    for entry_left in pending + later:
        advance(entry_left)
    total_blocks = len(done)
    for index in range(total_blocks - CROSS_LAG, total_blocks):
        combine(done[index])
    for index in range(total_blocks - STRIP_LAG, total_blocks):
        finish(done[index])

    cols = out.shape[1] // 4
    for which in range(4):
        for strip in range(ny):
            here = jnp.logical_and(jnp.logical_and(final_y == y, quarter == which), y == strip)

            @pl.when(jnp.logical_not(here))
            def _():
                piece_copy(own, which, strip).wait_recv()

        out[:, which * cols : (which + 1) * cols] = pieces[which]

    @pl.when(me < n_ctx - 1)
    def _():
        halo_copy(me + 1).wait_send()

    def drain_params(step, carry):
        param_copy(step, me, chip_at(step)).wait_send()
        relay_copy(step, chip_at(step)).wait_send()
        return carry

    own_across.wait_send()
    lax.fori_loop(1, n_chips, drain_params, 0)
    weight_copy(x_hi).wait_send()
    pair.wait_send()
    give.wait_send()

    each_target(lambda copy: copy.wait_send())

    @pl.when(x_hi == 0)
    def _():
        total_copy.wait_send()

    for step in range(far):
        for way in range(2):
            for part in ring_halves(way, step + 1):
                ring_copy(own, way, step, part).wait_send()
    for slot in range(nz):
        across_copy(own, slot).wait_send()

    def drain_blocks(block, carry):
        cross_copy(block).wait_send()
        for step in range(1, ny):
            strip_copy(block, y, lax.rem(y + step, ny)).wait_send()

        @pl.when(jnp.logical_not(stays(block)))
        def _():
            piece_copy(block, quarter, y).wait_send()

        return carry

    lax.fori_loop(0, per_x, drain_blocks, 0)


def per_device(n_ctx, n_tp, features, conv_weight, decay_rates, residues, skip_gain, out_weight):
    nz, ny = n_ctx // 4, n_tp // 2
    _, rows, width = features.shape
    modes, span = decay_rates.shape
    tiles, steps = width // LANES, rows // ROWS
    cols = out_weight.shape[1]
    blocks = 2 * nz
    tile_state = (tiles, modes, LANES)
    row_state = (tiles, modes, ROWS, LANES)
    half_state = (tiles // 2, modes, LANES)
    dma = pltpu.SemaphoreType.DMA
    vmem = pl.BlockSpec(memory_space=pltpu.VMEM)
    return pl.pallas_call(
        functools.partial(kernel, (nz, ny, n_ctx, n_tp)),
        out_shape=jax.ShapeDtypeStruct((rows, 4 * cols), BF16),
        in_specs=[pl.BlockSpec(memory_space=pltpu.HBM)] * 6,
        out_specs=vmem,
        scratch_shapes=[
            pltpu.VMEM(features.shape, BF16),
            pltpu.VMEM(conv_weight.shape[:2] + (width,), F32),
            pltpu.VMEM((modes, span), F32),
            pltpu.VMEM((modes, span), F32),
            pltpu.VMEM((1, span), F32),
            pltpu.VMEM((modes, LANES), F32),
            pltpu.VMEM((n_ctx, modes, LANES), F32),
            pltpu.VMEM((3, 16, width), BF16),
            pltpu.VMEM((3, rows, LANES), F32),
            pltpu.VMEM((tiles, steps, ROWS, LANES), F32),
            pltpu.VMEM((tiles, steps, ROWS, LANES), F32),
            pltpu.VMEM(tile_state, F32),
            pltpu.VMEM(tile_state, F32),
            pltpu.VMEM(tile_state, F32),
            pltpu.VMEM((DECAY_STEPS,) + tile_state, F32),
            pltpu.VMEM(tile_state, F32),
            pltpu.VMEM(tile_state, F32),
            pltpu.VMEM(half_state, F32),
            pltpu.VMEM((n_ctx // 2,) + half_state, F32),
            pltpu.VMEM(half_state, F32),
            pltpu.VMEM(tile_state, F32),
            pltpu.VMEM(row_state, F32),
            pltpu.VMEM(row_state, F32),
            pltpu.VMEM((rows, LANES), F32),
            pltpu.VMEM((blocks, rows, width), BF16),
            pltpu.VMEM((2, width, cols), BF16),
            pltpu.VMEM((blocks, rows, cols), F32),
            pltpu.VMEM((blocks, rows, cols), BF16),
            pltpu.VMEM((blocks, rows, cols), BF16),
            pltpu.VMEM((blocks, rows, cols), BF16),
            pltpu.VMEM((ny, blocks, rows // ny, cols), BF16),
            pltpu.VMEM((blocks, rows // ny, cols), BF16),
            pltpu.VMEM((4, rows, cols), BF16),
            dma((6,)),
            dma((2,)),
            dma((2,)),
            dma((4,)),
            dma((n_ctx,)),
            dma((n_ctx,)),
            dma((n_ctx // 2,)),
            dma((n_ctx // 2,)),
            dma((2,)),
            dma((2, nz // 2, 2)),
            dma((nz,)),
            dma((blocks, 2)),
            dma((blocks,)),
            dma((blocks,)),
            dma((blocks, ny)),
            dma((ny, blocks)),
            dma((blocks,)),
            dma((4, ny)),
        ],
        compiler_params=pltpu.CompilerParams(
            collective_id=0, has_side_effects=True, vmem_limit_bytes=67_000_000
        ),
    )(features, conv_weight, decay_rates, residues, skip_gain[None, :], out_weight)


def solution(mesh):
    in_specs = (
        P(None, "ctx", "tp"),
        P(),
        P(None, ("tp", "ctx")),
        P(None, ("tp", "ctx")),
        P(("tp", "ctx")),
        P("tp", "ctx"),
    )
    return jax.shard_map(
        functools.partial(per_device, mesh.shape["ctx"], mesh.shape["tp"]),
        mesh=mesh,
        in_specs=in_specs,
        out_specs=P("ctx", "tp"),
        check_vma=False,
    )
```

```python
import functools

import jax
import jax.numpy as jnp
from jax import lax
from jax.experimental import pallas as pl
from jax.experimental.pallas import tpu as pltpu
from jax.sharding import PartitionSpec as P

MESH = pl.DeviceIdType.MESH
F32 = jnp.float32
BF16 = jnp.bfloat16
LANES = 128
ROWS = 8
CROSS_LAG = 3
STRIP_LAG = 6
DECAY_STEPS = 6


def row_of(tile, index):
    return jnp.broadcast_to(tile[index : index + 1, :], (ROWS, LANES))


def kernel(
    dims,
    features,
    all_taps,
    decay_rates,
    residues,
    skip_gain,
    weight,
    out,
    feats,
    conv_weight,
    own_rates,
    own_residues,
    own_skip,
    pack,
    params,
    halo,
    plain,
    gate_in,
    query,
    rates,
    gains,
    skips,
    decays,
    ends,
    ends_other,
    chip_end,
    chip_ends,
    plane_total,
    carried,
    entry,
    entry_decay,
    gated_plain,
    gated,
    weights,
    kept,
    crossing,
    crossed,
    summed,
    strips,
    mixed,
    pieces,
    fetch_sem,
    halo_sem,
    weight_sem,
    pair_sem,
    param_send,
    param_recv,
    chip_send,
    chip_recv,
    plane_sem,
    ring_send,
    across_send,
    gated_recv,
    cross_send,
    cross_recv,
    strip_send,
    strip_recv,
    piece_send,
    piece_recv,
):
    nz, ny, n_ctx, n_tp = dims
    per_x = 2 * nz
    modes = rates.shape[1]
    tiles = feats.shape[2] // LANES
    half_tiles = tiles // 2
    steps = feats.shape[1] // ROWS
    width = feats.shape[2]
    me = lax.axis_index("ctx")
    tp = lax.axis_index("tp")
    core = lax.rem(me, 2)
    chip = lax.div(me, 2)
    x_hi = lax.div(me, per_x)
    z = lax.rem(chip, nz)
    x_lo = lax.div(tp, ny)
    y = lax.rem(tp, ny)
    own = lax.rem(me, per_x)
    partner = me + 1 - 2 * core
    x_partner = lax.rem(me + per_x, n_ctx)
    final_y = lax.div(z, 2)
    quarter = lax.rem(me, 4)
    strip_rows = feats.shape[1] // ny

    def remote(src, dst, send, recv, device):
        return pltpu.make_async_remote_copy(
            src_ref=src, dst_ref=dst, send_sem=send, recv_sem=recv, device_id=device, device_id_type=MESH
        )

    own_lanes = pl.ds(pl.multiple_of(tp * width, width), width)
    fetches = [
        pltpu.make_async_copy(src, dst, fetch_sem.at[slot])
        for slot, (src, dst) in enumerate(
            [
                (decay_rates, own_rates),
                (residues, own_residues),
                (skip_gain, own_skip),
                (features, feats),
                (all_taps.at[:, :, own_lanes], conv_weight),
                (weight, weights.at[x_hi]),
            ]
        )
    ]
    for fetch in fetches:
        fetch.start()

    barrier = pltpu.get_barrier_semaphore()

    def greet_ctx(step, carry):
        pl.semaphore_signal(barrier, inc=1, device_id={"ctx": lax.rem(me + step, n_ctx)}, device_id_type=MESH)
        return carry

    def greet_tp(step, carry):
        pl.semaphore_signal(barrier, inc=1, device_id={"tp": lax.rem(tp + step, n_tp)}, device_id_type=MESH)
        return carry

    lax.fori_loop(1, n_ctx, greet_ctx, 0)
    lax.fori_loop(1, n_tp, greet_tp, 0)
    for other_y in range(1, ny):
        for which in range(4):
            pl.semaphore_signal(
                barrier,
                inc=1,
                device_id={"ctx": x_hi * per_x + 4 * y + which, "tp": x_lo * ny + lax.rem(y + other_y, ny)},
                device_id_type=MESH,
            )

    for fetch in fetches:
        fetch.wait()
    modes_shape = own_rates.shape
    packed = jnp.concatenate(
        [
            own_rates[...],
            own_residues[...],
            jnp.broadcast_to(own_skip[...], modes_shape),
            jnp.zeros((modes_shape[0], LANES - 3 * modes_shape[1]), F32),
        ],
        axis=1,
    )
    pack[...] = packed
    params[me] = packed

    pl.semaphore_wait(barrier, n_ctx + n_tp - 2 + jnp.where(final_y != y, per_x, 0))

    last_rows = pl.ds(feats.shape[1] - halo.shape[1], halo.shape[1])

    def halo_copy(device):
        return remote(feats.at[:, last_rows, :], halo, halo_sem.at[0], halo_sem.at[1], {"ctx": device})

    def param_copy(step, source, device):
        return remote(pack, params.at[source], param_send.at[step], param_recv.at[source], {"ctx": device})

    def weight_copy(slot):
        return remote(weights.at[slot], weights.at[slot], weight_sem.at[0], weight_sem.at[1], {"ctx": x_partner})

    @pl.when(me < n_ctx - 1)
    def _():
        halo_copy(me + 1).start()

    n_chips = n_ctx // 2

    def chip_at(step):
        return 2 * lax.rem(chip + step, n_chips) + core

    def send_params(step, carry):
        param_copy(step, me, chip_at(step)).start()
        return carry

    own_across = remote(pack, params.at[me], param_send.at[0], param_recv.at[me], {"ctx": partner})
    own_across.start()
    lax.fori_loop(1, n_chips, send_params, 0)

    @pl.when(me > 0)
    def _():
        halo_copy(me - 1).wait_recv()

    @pl.when(me == 0)
    def _():
        halo[...] = jnp.zeros_like(halo)

    row = lax.broadcasted_iota(jnp.int32, (ROWS, LANES), 0)
    lane_group = lax.broadcasted_iota(jnp.int32, (modes, LANES), 1) // (width // n_ctx)
    groups = LANES * n_ctx // width

    def short_conv(tile, carry):
        lanes = pl.ds(pl.multiple_of(tile * LANES, LANES), LANES)
        filtered = []
        for kind in range(3):
            plain[kind] = feats[kind, :, lanes].astype(F32)
            before = halo[kind, :, lanes].astype(F32)
            taps = conv_weight[kind, :, lanes]
            tap = [row_of(taps, j) for j in range(3)]
            now = [plain[kind, pl.ds(step, ROWS, stride=steps), :] for step in range(steps)]
            last = halo.shape[1] - 1
            one = jnp.where(row == 0, row_of(before, last), pltpu.roll(now[steps - 1], 1, 0))
            two = jnp.where(row == 0, row_of(before, last - 1), pltpu.roll(now[steps - 2], 1, 0))
            chain = [two, one] + now
            filtered.append(
                [tap[0] * chain[s + 2] + tap[1] * chain[s + 1] + tap[2] * chain[s] for s in range(steps)]
            )
        for step in range(steps):
            query[tile, step] = filtered[0][step]
            gate_in[tile, step] = (filtered[1][step] * filtered[2][step]).astype(BF16).astype(F32)
        return carry

    lax.fori_loop(0, tiles, short_conv, 0)

    def relay_copy(step, source):
        return remote(
            params.at[source],
            params.at[source],
            param_send.at[n_chips + step],
            param_recv.at[source],
            {"ctx": partner},
        )

    def relay_params(step, carry):
        source = chip_at(step)
        param_copy(step, source, source).wait_recv()
        relay_copy(step, source).start()
        return carry

    lax.fori_loop(1, n_chips, relay_params, 0)

    def wait_params(step, carry):
        relay_copy(0, chip_at(step) + 1 - 2 * core).wait_recv()
        return carry

    lax.fori_loop(0, n_chips, wait_params, 0)

    span = width // n_ctx

    def local_states(tile, carry):
        rate = jnp.zeros((modes, LANES), F32)
        residue = jnp.zeros((modes, LANES), F32)
        skip = jnp.zeros((modes, LANES), F32)
        for group in range(groups):
            piece = params[tile * groups + group]
            at = lambda which: pltpu.roll(piece, (group - which) * span % LANES, 1)
            mine = lane_group == group
            rate = jnp.where(mine, at(0), rate)
            residue = jnp.where(mine, at(1), residue)
            skip = jnp.where(mine, at(2), skip)
        rates[tile] = rate
        gains[tile] = residue * jnp.sqrt(2.0 * rate)
        skips[tile] = skip
        power = []
        for slot, tokens in enumerate((1, steps, 2 * steps, 4 * steps, 8 * steps, 16 * steps)):
            value = jnp.exp(-float(tokens) * rate)
            power.append(value)
            decays[slot, tile] = value
        signal = [gate_in[tile, step] for step in range(steps)]
        row_tokens = row.astype(F32) * float(steps)
        for mode in range(modes):
            decay = row_of(power[0], mode)
            state = signal[0]
            for step in range(1, steps):
                state = decay * state + signal[step]
            for slot in range(3):
                reach = 1 << slot
                factor = jnp.where(row >= reach, row_of(power[1 + slot], mode), 0.0)
                state = state + factor * pltpu.roll(state, reach, 0)
            ends[tile, mode : mode + 1, :] = state[ROWS - 1 :, :]
            entry[tile, mode] = jnp.where(row >= 1, pltpu.roll(state, 1, 0), 0.0)
            entry_decay[tile, mode] = jnp.exp(-row_tokens * row_of(rate, mode))
        return carry

    lax.fori_loop(0, tiles, local_states, 0)

    pair = remote(ends, ends_other, pair_sem.at[0], pair_sem.at[1], {"ctx": partner})
    pair.start()
    pair.wait_recv()
    half = pl.ds(core * half_tiles, half_tiles)
    mine, other = ends[half], ends_other[half]
    first = jnp.where(core == 0, mine, other)
    second = jnp.where(core == 0, other, mine)
    chip_end[...] = decays[4, half] * first + second

    def chip_copy(source, target):
        return remote(
            chip_end, chip_ends.at[source], chip_send.at[target], chip_recv.at[source], {"ctx": 2 * target + core}
        )

    def each_target(act):
        def body(step, carry):
            to_z = lax.rem(z + step, nz)

            @pl.when(jnp.logical_or(x_hi == 0, to_z > z))
            def _():
                act(chip_copy(chip, x_hi * nz + to_z))

            return carry

        lax.fori_loop(1, nz, body, 0)

    each_target(lambda copy: copy.start())
    weight_copy(x_hi).start()
    long_decay = decays[5, half]
    total_copy = remote(plane_total, plane_total, plane_sem.at[0], plane_sem.at[1], {"ctx": x_partner})

    def take_chip(source, state):
        total, power = state
        chip_copy(source, source).wait_recv()
        return total * long_decay + chip_ends[source], power * long_decay

    nothing = jnp.zeros(chip_end.shape, F32)
    before_here, reach_back = lax.fori_loop(x_hi * nz, chip, take_chip, (nothing, nothing + 1.0))
    carried[half] = before_here

    @pl.when(x_hi == 1)
    def _():
        total_copy.wait_recv()
        carried[half] = carried[half] + reach_back * plane_total[...]

    give = remote(carried.at[half], carried.at[half], pair_sem.at[2], pair_sem.at[3], {"ctx": partner})
    give.start()

    @pl.when(x_hi == 0)
    def _():
        through_here = before_here * long_decay + chip_end[...]
        whole, _ = lax.fori_loop(chip + 1, nz, take_chip, (through_here, nothing))
        plane_total[...] = whole
        total_copy.start()

    other_half = pl.ds((1 - core) * half_tiles, half_tiles)
    remote(carried.at[half], carried.at[other_half], pair_sem.at[2], pair_sem.at[3], {"ctx": partner}).wait_recv()

    def long_conv(tile, carry):
        into_chip = carried[tile]
        into = jnp.where(core == 0, into_chip, decays[4, tile] * into_chip + ends_other[tile])
        power, gain = decays[0, tile], gains[tile]
        decay = [row_of(power, m) for m in range(modes)]
        weigh = [row_of(gain, m) for m in range(modes)]
        skip = row_of(skips[tile], 0)
        state = [entry[tile, m] + entry_decay[tile, m] * row_of(into, m) for m in range(modes)]
        for step in range(steps):
            signal = gate_in[tile, step]
            total = skip * signal
            for m in range(modes):
                state[m] = decay[m] * state[m] + signal
                total = total + weigh[m] * state[m]
            long_out = total.astype(BF16).astype(F32)
            gated_plain[pl.ds(step, ROWS, stride=steps), :] = query[tile, step] * long_out
        lanes = pl.ds(pl.multiple_of(tile * LANES, LANES), LANES)
        gated[own, :, lanes] = gated_plain[...].astype(BF16)
        return carry

    lax.fori_loop(0, tiles, long_conv, 0)

    def ring_device(to_z):
        return {"ctx": x_hi * per_x + 2 * to_z + core}

    devices = [ring_device(lax.rem(z + 1, nz)), ring_device(lax.rem(z + nz - 1, nz))]
    far = nz // 2
    half_rows = feats.shape[1] // 2

    def ring_halves(way, step):
        return [way, 1 - way] if step < far else [way]

    def ring_block(way, step):
        return 2 * lax.rem(z + (nz - step if way == 0 else step), nz) + core

    def ring_copy(block, way, step, part):
        rows = pl.ds(part * half_rows, half_rows)
        return remote(
            gated.at[block, rows],
            gated.at[block, rows],
            ring_send.at[way, step, part],
            gated_recv.at[block, part],
            devices[way],
        )

    def across_copy(block, slot):
        return remote(
            gated.at[block], gated.at[block], across_send.at[slot], gated_recv.at[block, 0], {"ctx": partner}
        )

    def cross_copy(block):
        return remote(
            crossing.at[block],
            crossed.at[block],
            cross_send.at[block],
            cross_recv.at[block],
            {"tp": (1 - x_lo) * ny + y},
        )

    def strip_copy(block, source, target):
        rows = pl.ds(pl.multiple_of(target * strip_rows, strip_rows), strip_rows)
        return remote(
            summed.at[block, rows],
            strips.at[source, block],
            strip_send.at[block, target],
            strip_recv.at[source, block],
            {"tp": x_lo * ny + target},
        )

    def piece_copy(block, which, strip):
        rows = pl.ds(pl.multiple_of(strip * strip_rows, strip_rows), strip_rows)
        return remote(
            mixed.at[block],
            pieces.at[which, rows],
            piece_send.at[block],
            piece_recv.at[which, strip],
            {"ctx": x_hi * per_x + block, "tp": x_lo * ny + final_y},
        )

    def stays(block):
        return jnp.logical_and(block == own, final_y == y)

    def multiply(block):
        value = jnp.dot(gated[block], weights[1 - x_lo], preferred_element_type=F32)
        crossing[block] = value.astype(BF16)
        cross_copy(block).start()
        kept[block] = jnp.dot(gated[block], weights[x_lo], preferred_element_type=F32)

    def combine(block):
        cross_copy(block).wait_recv()
        summed[block] = (kept[block] + crossed[block].astype(F32)).astype(BF16)
        for step in range(1, ny):
            strip_copy(block, y, lax.rem(y + step, ny)).start()

    def finish(block):
        own_rows = pl.ds(pl.multiple_of(y * strip_rows, strip_rows), strip_rows)
        total = summed[block, own_rows].astype(F32)
        for step in range(1, ny):
            source = lax.rem(y + step, ny)
            strip_copy(block, source, y).wait_recv()
            total = total + strips[source, block].astype(F32)
        value = total.astype(BF16)

        @pl.when(stays(block))
        def _():
            pieces[quarter, own_rows] = value

        @pl.when(jnp.logical_not(stays(block)))
        def _():
            mixed[block] = value
            piece_copy(block, quarter, y).start()

    for way in range(2):
        for part in ring_halves(way, 1):
            ring_copy(own, way, 0, part).start()
    across_copy(own, 0).start()
    weight_copy(1 - x_hi).wait_recv()

    done = []

    def advance(entry):
        block, waits = entry
        if waits:
            across_copy(block, 0).wait_recv()
        multiply(block)
        done.append(block)
        if len(done) > CROSS_LAG:
            combine(done[-1 - CROSS_LAG])
        if len(done) > STRIP_LAG:
            finish(done[-1 - STRIP_LAG])

    def other(block):
        return block + 1 - 2 * core

    pending = [(own, False)]
    later = [(other(own), True)]
    for step in range(1, far + 1):
        ways = [0, 1]
        arrived = [ring_block(way, step) for way in ways]
        if step == far:
            for waiting in pending + later:
                advance(waiting)
            pending, later = [], []
        for turn in range(len(ring_halves(0, step))):
            for way in ways:
                part = ring_halves(way, step)[turn]
                ring_copy(arrived[way], way, 0, part).wait_recv()
                if step < far and part in ring_halves(way, step + 1):
                    ring_copy(arrived[way], way, step, part).start()
            if turn == 0:
                for _ in range(min(2, len(pending))):
                    advance(pending.pop(0))
        blocks = arrived if step < far else arrived[:1]
        for index, block in enumerate(blocks):
            across_copy(block, 2 * step - 1 + index).start()
        while pending:
            advance(pending.pop(0))
        pending = later + [(block, False) for block in blocks]
        later = [(other(block), True) for block in blocks]
    for entry_left in pending + later:
        advance(entry_left)
    total_blocks = len(done)
    for index in range(total_blocks - CROSS_LAG, total_blocks):
        combine(done[index])
    for index in range(total_blocks - STRIP_LAG, total_blocks):
        finish(done[index])

    cols = out.shape[1] // 4
    for which in range(4):
        for strip in range(ny):
            here = jnp.logical_and(jnp.logical_and(final_y == y, quarter == which), y == strip)

            @pl.when(jnp.logical_not(here))
            def _():
                piece_copy(own, which, strip).wait_recv()

        out[:, which * cols : (which + 1) * cols] = pieces[which]

    @pl.when(me < n_ctx - 1)
    def _():
        halo_copy(me + 1).wait_send()

    def drain_params(step, carry):
        param_copy(step, me, chip_at(step)).wait_send()
        relay_copy(step, chip_at(step)).wait_send()
        return carry

    own_across.wait_send()
    lax.fori_loop(1, n_chips, drain_params, 0)
    weight_copy(x_hi).wait_send()
    pair.wait_send()
    give.wait_send()

    each_target(lambda copy: copy.wait_send())

    @pl.when(x_hi == 0)
    def _():
        total_copy.wait_send()

    for step in range(far):
        for way in range(2):
            for part in ring_halves(way, step + 1):
                ring_copy(own, way, step, part).wait_send()
    for slot in range(nz):
        across_copy(own, slot).wait_send()

    def drain_blocks(block, carry):
        cross_copy(block).wait_send()
        for step in range(1, ny):
            strip_copy(block, y, lax.rem(y + step, ny)).wait_send()

        @pl.when(jnp.logical_not(stays(block)))
        def _():
            piece_copy(block, quarter, y).wait_send()

        return carry

    lax.fori_loop(0, per_x, drain_blocks, 0)


def per_device(n_ctx, n_tp, features, conv_weight, decay_rates, residues, skip_gain, out_weight):
    nz, ny = n_ctx // 4, n_tp // 2
    _, rows, width = features.shape
    modes, span = decay_rates.shape
    tiles, steps = width // LANES, rows // ROWS
    cols = out_weight.shape[1]
    blocks = 2 * nz
    tile_state = (tiles, modes, LANES)
    row_state = (tiles, modes, ROWS, LANES)
    half_state = (tiles // 2, modes, LANES)
    dma = pltpu.SemaphoreType.DMA
    vmem = pl.BlockSpec(memory_space=pltpu.VMEM)
    return pl.pallas_call(
        functools.partial(kernel, (nz, ny, n_ctx, n_tp)),
        out_shape=jax.ShapeDtypeStruct((rows, 4 * cols), BF16),
        in_specs=[pl.BlockSpec(memory_space=pltpu.HBM)] * 6,
        out_specs=vmem,
        scratch_shapes=[
            pltpu.VMEM(features.shape, BF16),
            pltpu.VMEM(conv_weight.shape[:2] + (width,), F32),
            pltpu.VMEM((modes, span), F32),
            pltpu.VMEM((modes, span), F32),
            pltpu.VMEM((1, span), F32),
            pltpu.VMEM((modes, LANES), F32),
            pltpu.VMEM((n_ctx, modes, LANES), F32),
            pltpu.VMEM((3, 16, width), BF16),
            pltpu.VMEM((3, rows, LANES), F32),
            pltpu.VMEM((tiles, steps, ROWS, LANES), F32),
            pltpu.VMEM((tiles, steps, ROWS, LANES), F32),
            pltpu.VMEM(tile_state, F32),
            pltpu.VMEM(tile_state, F32),
            pltpu.VMEM(tile_state, F32),
            pltpu.VMEM((DECAY_STEPS,) + tile_state, F32),
            pltpu.VMEM(tile_state, F32),
            pltpu.VMEM(tile_state, F32),
            pltpu.VMEM(half_state, F32),
            pltpu.VMEM((n_ctx // 2,) + half_state, F32),
            pltpu.VMEM(half_state, F32),
            pltpu.VMEM(tile_state, F32),
            pltpu.VMEM(row_state, F32),
            pltpu.VMEM(row_state, F32),
            pltpu.VMEM((rows, LANES), F32),
            pltpu.VMEM((blocks, rows, width), BF16),
            pltpu.VMEM((2, width, cols), BF16),
            pltpu.VMEM((blocks, rows, cols), F32),
            pltpu.VMEM((blocks, rows, cols), BF16),
            pltpu.VMEM((blocks, rows, cols), BF16),
            pltpu.VMEM((blocks, rows, cols), BF16),
            pltpu.VMEM((ny, blocks, rows // ny, cols), BF16),
            pltpu.VMEM((blocks, rows // ny, cols), BF16),
            pltpu.VMEM((4, rows, cols), BF16),
            dma((6,)),
            dma((2,)),
            dma((2,)),
            dma((4,)),
            dma((n_ctx,)),
            dma((n_ctx,)),
            dma((n_ctx // 2,)),
            dma((n_ctx // 2,)),
            dma((2,)),
            dma((2, nz // 2, 2)),
            dma((nz,)),
            dma((blocks, 2)),
            dma((blocks,)),
            dma((blocks,)),
            dma((blocks, ny)),
            dma((ny, blocks)),
            dma((blocks,)),
            dma((4, ny)),
        ],
        compiler_params=pltpu.CompilerParams(
            collective_id=0, has_side_effects=True, vmem_limit_bytes=67_000_000
        ),
    )(features, conv_weight, decay_rates, residues, skip_gain[None, :], out_weight)


def solution(mesh):
    in_specs = (
        P(None, "ctx", "tp"),
        P(),
        P(None, ("tp", "ctx")),
        P(None, ("tp", "ctx")),
        P(("tp", "ctx")),
        P("tp", "ctx"),
    )
    return jax.shard_map(
        functools.partial(per_device, mesh.shape["ctx"], mesh.shape["tp"]),
        mesh=mesh,
        in_specs=in_specs,
        out_specs=P("ctx", "tp"),
        check_vma=False,
    )
```
